32 devices in a mesh: rep: 2 (over core), mp: 16 (over z, y, x).
Axes of the slice: x: 2, y: 2, z: 4, core: 2. Of those that a mesh axis runs over, the one named last changes fastest.
Arguments:
- lookup_block: int32 [2, 2048, 16, 4], P(None, ('rep', 'mp')), may hold values from 0 to 9
- lookup_offset: int32 [2, 2048, 16, 4], P(None, ('rep', 'mp')), may hold values from 0 to 63
- interaction_grad: bfloat16 [2, 2048, 16, 16], P(None, ('rep', 'mp')), may hold values from -4 to 4
- table: bfloat16 [49152, 256], P('mp'), may hold values from -0.3125 to 0.3125
- adagrad_state: float32 [49152], P('mp'), may hold values from 0.05 to 2
- touched_blocks: int32 [16, 10], P('mp'), may hold values from 0 to 47, as said below
- dither: int32 [16, 640, 256], P('mp'), may hold values from 0 to 32767
Outputs:
- new_table: bfloat16 [49152, 256], P('mp')
- new_state: float32 [49152], P('mp')
The draws below stay inside these ranges and needn't reach their ends.
Inputs may be any that keep to these rules, and one draw needn't show every extreme that they name: `touched_blocks`: each row names 10 different row blocks.
All inputs are finite; a program needn't handle non-finite values.
Results may differ from the reference program's by a relative error of at most 0.00055.
The reference program's roundings to bfloat16 on the way count: a program that leaves them out, or rounds other values in their place, can miss the bound.
Values may be sent and summed in bfloat16 or wider, within the bound.
A program may use at most 128 MiB of HBM per device.

```python
import math
import jax
import jax.numpy as jnp
import numpy as np
from jax import lax

E = 256
MICRO = 2
BAG = 4
BLOCK = 64
TOUCH = 10
NBLK = 48
FEATURES = 16
SAMPLES = 2048
ROWS = 49152
N_MP = 16


def draw_touched_blocks(key, part):
    feature_keys = jax.random.split(jax.random.fold_in(key, 17), N_MP)

    def one_table(table_key):
        return jax.random.permutation(table_key, NBLK)[:TOUCH]
    return jax.vmap(one_table)(feature_keys).astype(jnp.int32)


def set_ends(values, stream_key, least, largest):
    extent = values.shape
    index_at = [jax.random.randint(jax.random.fold_in(stream_key, axis), (), 0, extent[axis]) for axis in range(len(extent))]
    values = values.at[tuple(index_at)].set(least)
    longest = extent.index(max(extent))
    index_at[longest] = (index_at[longest] + 1) % extent[longest]
    return values.at[tuple(index_at)].set(largest)


def block_scale(stream_key, shape, cuts, least, largest):
    level = 1.0
    for axis_at, parts in cuts:
        heights = jax.random.uniform(jax.random.fold_in(jax.random.fold_in(stream_key, 6), axis_at), (parts,), jnp.float32, least / len(cuts), largest / len(cuts))
        level = level * jnp.repeat(jnp.exp(heights), shape[axis_at] // parts).reshape((-1,) + (1,) * (len(shape) - 1 - axis_at))
    return level


def rank_table(number_of, skew):
    loads = [(1 << 20) // math.isqrt(grade ** skew) + 1 for grade in range(1, number_of + 1)]
    scale = 1 + sum(loads) // (1 << 30)
    return np.cumsum(np.array([max(1, weight // scale) for weight in loads]))


def ranked(key, shape, number_of, skew):
    grid = rank_table(number_of, skew)
    lot = jax.random.randint(jax.random.fold_in(key, 1), shape, 0, int(grid[number_of - 1]))
    grade = jnp.searchsorted(jnp.asarray(grid, jnp.int32), lot, side="right")
    return jax.random.permutation(jax.random.fold_in(key, 2), number_of)[grade].astype(jnp.int32)


def scatter_about(own_key, dims, scale, most, shards=(), held_as=jnp.bfloat16):
    loudness = block_scale(own_key, dims, shards, -0.22, 0.18) if shards else 1.0
    array = jax.random.normal(own_key, dims, jnp.float32) * scale * loudness
    return jnp.minimum(jnp.maximum(array, -most), most).astype(held_as)


def setup_inputs(seed: int = 0) -> dict:
    splits = jax.random.split(jax.random.key(seed), 8)
    return {
        "lookup_block": set_ends(ranked(splits[0], (MICRO, SAMPLES, FEATURES, BAG), TOUCH, 1), jax.random.fold_in(splits[0], 3), 0, TOUCH - 1).astype(jnp.int32),
        "lookup_offset": set_ends(jax.random.randint(splits[1], (MICRO, SAMPLES, FEATURES, BAG), 0, BLOCK), jax.random.fold_in(splits[1], 1), 0, BLOCK - 1).astype(jnp.int32),
        "interaction_grad": scatter_about(splits[2], (MICRO, SAMPLES, FEATURES, FEATURES), (FEATURES ** -0.5), 4.0, ((1, 32),)),
        "table": scatter_about(splits[3], (ROWS, E), 0.02, 0.3125, ((0, 16),)),
        "adagrad_state": jnp.clip(jnp.exp(math.log(2.0) - 3.6888794 * jax.random.uniform(splits[4], (ROWS,), jnp.float32) ** block_scale(splits[4], (ROWS,), ((0, 16),), -0.2, 0.2)), 0.05, 2.0),
        "touched_blocks": draw_touched_blocks(jax.random.fold_in(splits[7], 71), 0),
        "dither": set_ends(jax.random.randint(splits[6], (FEATURES, TOUCH * BLOCK, E), 0, 32768), jax.random.fold_in(splits[6], 1), 0, 32767).astype(jnp.int32),
    }


LEARN_RATE = 0.1
POOL_DECAY = 0.5
DITHER_UNIT = 2.0 ** (-15)
SMALLEST = 2.0 ** (-14)

def dither_round(weights, dither_bits):
    magnitude = jnp.maximum(jnp.abs(weights), SMALLEST)
    spacing = jnp.exp2(jnp.floor(jnp.log2(magnitude)) - 7.0)
    grid_level = jnp.floor(weights / spacing + dither_bits.astype(jnp.float32) * DITHER_UNIT)
    return (grid_level * spacing).astype(jnp.bfloat16)

def pairwise(pooled_rows, cotangent):
    pooled_wide = pooled_rows.astype(jnp.float32)
    cot_wide = cotangent.astype(jnp.float32)
    forward = jnp.einsum('bfg,bge->bfe', cot_wide, pooled_wide)
    backward = jnp.einsum('bgf,bge->bfe', cot_wide, pooled_wide)
    return (forward + backward + POOL_DECAY * pooled_wide).astype(jnp.bfloat16)

def reference(lookup_block, lookup_offset, interaction_grad, table, adagrad_state, touched_blocks, dither):
    slab_size = TOUCH * BLOCK
    table_blocks = table.reshape(N_MP, NBLK, BLOCK, E)
    feature_ids = jnp.arange(N_MP, dtype=jnp.int32)[:, None]
    chosen = table_blocks[feature_ids, touched_blocks]
    slab_table = chosen.reshape(N_MP * slab_size, E)
    feature_base = (jnp.arange(N_MP, dtype=jnp.int32) * slab_size)[None, None, :, None]
    slab_index = (lookup_block * BLOCK + lookup_offset + feature_base).astype(jnp.int32)
    sample_block = math.gcd(256, SAMPLES)
    steps_count = MICRO * SAMPLES // sample_block
    blocked_index = slab_index.reshape(steps_count, sample_block, N_MP, BAG)
    blocked_cot = interaction_grad.reshape(steps_count, sample_block, N_MP, N_MP)

    def accumulate(carry, pieces):
        index_piece, cot_piece = pieces
        gathered = slab_table[index_piece].astype(jnp.float32)
        pooled_rows = lax.optimization_barrier(jnp.sum(gathered, axis=2)).astype(jnp.bfloat16)
        back_rows = pairwise(pooled_rows, cot_piece).astype(jnp.float32)
        spread = jnp.broadcast_to(back_rows[:, :, None, :], gathered.shape).reshape(-1, E)
        carry = carry + jax.ops.segment_sum(spread, index_piece.reshape(-1), num_segments=N_MP * slab_size)
        return (carry, None)
    start_grad = jnp.zeros((N_MP * slab_size, E), jnp.float32)
    slab_grad, _ = lax.scan(accumulate, start_grad, (blocked_index, blocked_cot))
    state_blocks = adagrad_state.reshape(N_MP, NBLK, BLOCK)
    state_slab = state_blocks[feature_ids, touched_blocks].reshape(N_MP * slab_size)
    state_next = state_slab + lax.optimization_barrier(jnp.mean(slab_grad * slab_grad, axis=-1))
    moved = slab_table.astype(jnp.float32) - LEARN_RATE * slab_grad / (jnp.sqrt(state_next) + 1e-08)[:, None]
    rounded = dither_round(moved, dither.reshape(N_MP * slab_size, E))
    new_table = table_blocks.at[feature_ids, touched_blocks].set(rounded.reshape(N_MP, TOUCH, BLOCK, E))
    new_state = state_blocks.at[feature_ids, touched_blocks].set(state_next.reshape(N_MP, TOUCH, BLOCK))
    return (new_table.reshape(ROWS, E), new_state.reshape(ROWS))
```

```python
import functools

import jax
import jax.numpy as jnp
from jax import lax
from jax.experimental import pallas as pl
from jax.experimental.pallas import tpu as pltpu
from jax.sharding import PartitionSpec as P

BLOCK = 64
LEARN_RATE = 0.1
POOL_DECAY = 0.5
DITHER_UNIT = 2.0 ** (-15)
SMALLEST = 2.0 ** (-14)
MESH = pl.DeviceIdType.MESH


def dither_round(weights, dither_bits):
    magnitude = jnp.maximum(jnp.abs(weights), SMALLEST)
    spacing = jnp.exp2(jnp.floor(jnp.log2(magnitude)) - 7.0)
    grid_level = jnp.floor(weights / spacing + dither_bits.astype(jnp.float32) * DITHER_UNIT)
    return (grid_level * spacing).astype(jnp.bfloat16)


def step_kernel(
    n,
    rows_ref,
    w_ref,
    slab_ref,
    state_ref,
    dither_ref,
    out_ref,
    state_out_ref,
    rows_all,
    w_other,
    slab_t,
    pooled_out,
    pooled_in,
    grad_out,
    grad_in,
    total,
    squares,
    rows_new,
    small_sem,
    rows_send,
    rows_recv,
    pooled_send,
    pooled_recv,
    grad_send,
    grad_recv,
):
    me = lax.axis_index("mp")
    half = lax.axis_index("rep")
    bags, samples = rows_ref.shape[1:]
    slab_size = slab_ref.shape[0]
    width = slab_t.shape[0]
    columns = pl.ds(pl.multiple_of(half * width, width), width)

    def at(peer):
        return {"device_id": (half, peer), "device_id_type": MESH}

    partner = {"device_id": (1 - half, me), "device_id_type": MESH}

    def peer_of(step):
        return lax.rem(me + step, n)

    def each_peer(body):
        def run(step, carry):
            body(peer_of(step))
            return carry

        lax.fori_loop(1, n, run, 0)

    barrier = pltpu.get_barrier_semaphore()
    each_peer(lambda peer: pl.semaphore_signal(barrier, inc=1, **at(peer)))
    pl.semaphore_signal(barrier, inc=1, **partner)
    pl.semaphore_wait(barrier, n)

    def rows_copy(peer, slot):
        return pltpu.make_async_remote_copy(
            rows_ref.at[peer],
            rows_all.at[half, slot],
            rows_send.at[peer],
            rows_recv.at[slot],
            **at(peer),
        )

    each_peer(lambda peer: rows_copy(peer, me).start())
    own_rows = pltpu.make_async_copy(rows_ref.at[me], rows_all.at[half, me], small_sem.at[0])
    own_rows.start()
    w_copy = pltpu.make_async_remote_copy(
        w_ref, w_other, small_sem.at[1], small_sem.at[2], **partner
    )
    w_copy.start()
    slab_t[...] = slab_ref[:, columns].astype(jnp.float32).T.astype(jnp.bfloat16)
    total[...] = jnp.zeros_like(total)
    own_rows.wait()
    each_peer(lambda peer: rows_copy(peer, peer).wait_recv())
    swap = pltpu.make_async_remote_copy(
        rows_all.at[half], rows_all.at[half], small_sem.at[3], small_sem.at[4], **partner
    )
    swap.start()

    slab_row = lax.broadcasted_iota(jnp.int32, (slab_size, samples), 0)

    def hits(rep, peer):
        block = rows_all[rep, peer]
        counted = jnp.zeros((slab_size, samples), jnp.float32)
        for lookup in range(bags):
            counted = counted + jnp.where(slab_row == block[lookup : lookup + 1, :], 1.0, 0.0)
        return counted.astype(jnp.bfloat16)

    def pooled_copy(part, peer, slot):
        return pltpu.make_async_remote_copy(
            pooled_out.at[part, peer],
            pooled_in.at[part, slot],
            pooled_send.at[part, peer],
            pooled_recv.at[part, slot],
            **at(peer),
        )

    def grad_copy(part, peer, slot):
        return pltpu.make_async_remote_copy(
            grad_out.at[part, peer],
            grad_in.at[part, slot],
            grad_send.at[part, peer],
            grad_recv.at[part, slot],
            **at(peer),
        )

    def pool(part, rep):
        def pooled(peer):
            return jnp.dot(
                slab_t[...], hits(rep, peer), preferred_element_type=jnp.float32
            ).astype(jnp.bfloat16)

        def send(peer):
            pooled_out[part, peer] = pooled(peer)
            pooled_copy(part, peer, me).start()

        each_peer(send)
        pooled_in[part, me] = pooled(me)

    def interact(part, weights):
        each_peer(lambda peer: pooled_copy(part, peer, peer).wait_recv())

        def mixed(feature):
            def add(other, carry):
                weight = weights[pl.ds(feature * n + other, 1), :]
                return carry + weight * pooled_in[part, other].astype(jnp.float32)

            zero = jnp.zeros((width, samples), jnp.float32)
            return lax.fori_loop(0, n, add, zero, unroll=4).astype(jnp.bfloat16)

        def send(peer):
            grad_out[part, peer] = mixed(peer)
            grad_copy(part, peer, me).start()

        each_peer(send)
        grad_in[part, me] = mixed(me)

    def collect(part, rep):
        def add(peer):
            total[...] += lax.dot_general(
                hits(rep, peer),
                grad_in[part, peer],
                (((1,), (1,)), ((), ())),
                preferred_element_type=jnp.float32,
            )

        def take(peer):
            grad_copy(part, peer, peer).wait_recv()
            add(peer)

        add(me)
        each_peer(take)

    pool(0, half)
    swap.wait_recv()
    pool(1, 1 - half)
    interact(0, w_ref)
    w_copy.wait_recv()
    interact(1, w_other)
    collect(0, half)
    collect(1, 1 - half)

    grad = total[...]
    squares[0] = jnp.sum((grad * grad).T, axis=0, keepdims=True)
    square_copy = pltpu.make_async_remote_copy(
        squares.at[0], squares.at[1], small_sem.at[5], small_sem.at[6], **partner
    )
    square_copy.start()
    square_copy.wait_recv()
    first = jnp.where(half == 0, squares[0], squares[1])
    second = jnp.where(half == 0, squares[1], squares[0])
    state_next = state_ref[...] + (first + second) / (2.0 * width)
    state_out_ref[...] = state_next
    divisor = jnp.broadcast_to(jnp.sqrt(state_next) + 1e-08, (width, slab_size)).T
    moved = slab_ref[:, columns].astype(jnp.float32) - LEARN_RATE * grad / divisor
    rows_new[0] = dither_round(moved, dither_ref[:, columns])
    new_copy = pltpu.make_async_remote_copy(
        rows_new.at[0], rows_new.at[1], small_sem.at[7], small_sem.at[8], **partner
    )
    new_copy.start()
    out_ref[:, columns] = rows_new[0]

    each_peer(lambda peer: rows_copy(peer, peer).wait_send())
    for part in range(2):
        each_peer(lambda peer: pooled_copy(part, peer, peer).wait_send())
        each_peer(lambda peer: grad_copy(part, peer, peer).wait_send())
    w_copy.wait_send()
    swap.wait_send()
    square_copy.wait_send()
    new_copy.wait()
    out_ref[:, pl.ds(pl.multiple_of((1 - half) * width, width), width)] = rows_new[1]


def fused_step(n, rows, weights, slab, state_row, dither):
    bags, samples = rows.shape[1:]
    slab_size, emb_width = slab.shape
    width = emb_width // 2
    dma = pltpu.SemaphoreType.DMA
    block = (2, n, width, samples)
    vmem = pl.BlockSpec(memory_space=pltpu.VMEM)
    return pl.pallas_call(
        functools.partial(step_kernel, n),
        out_shape=(
            jax.ShapeDtypeStruct((slab_size, emb_width), jnp.bfloat16),
            jax.ShapeDtypeStruct((1, slab_size), jnp.float32),
        ),
        in_specs=[vmem] * 5,
        out_specs=(vmem, vmem),
        scratch_shapes=[
            pltpu.VMEM((2, n, bags, samples), jnp.int32),
            pltpu.VMEM(weights.shape, jnp.float32),
            pltpu.VMEM((width, slab_size), jnp.bfloat16),
            pltpu.VMEM(block, jnp.bfloat16),
            pltpu.VMEM(block, jnp.bfloat16),
            pltpu.VMEM(block, jnp.bfloat16),
            pltpu.VMEM(block, jnp.bfloat16),
            pltpu.VMEM((slab_size, width), jnp.float32),
            pltpu.VMEM((2, 1, slab_size), jnp.float32),
            pltpu.VMEM((2, slab_size, width), jnp.bfloat16),
            dma((9,)),
            dma((n,)),
            dma((n,)),
            dma((2, n)),
            dma((2, n)),
            dma((2, n)),
            dma((2, n)),
        ],
        compiler_params=pltpu.CompilerParams(collective_id=0, has_side_effects=True),
        name="fused_step",
    )(rows, weights, slab, state_row, dither)


def per_device(
    lookup_block, lookup_offset, interaction_grad, table, adagrad_state, touched_blocks, dither
):
    micro_count, sample_count, feature_count, bag_count = lookup_block.shape
    n = lax.axis_size("mp")
    samples = micro_count * sample_count
    row_count, emb_width = table.shape
    touch_count = touched_blocks.shape[1]
    slab_size = touch_count * BLOCK
    rows = (lookup_block * BLOCK + lookup_offset).reshape(samples, feature_count * bag_count)
    rows = rows.T.reshape(feature_count, bag_count, samples)
    cot = interaction_grad.reshape(samples, feature_count, feature_count).astype(jnp.float32)
    weights = cot + jnp.swapaxes(cot, 1, 2) + POOL_DECAY * jnp.eye(feature_count)
    weights = weights.reshape(samples, feature_count * feature_count).T
    table_blocks = table.reshape(row_count // BLOCK, BLOCK, emb_width)
    slab = table_blocks[touched_blocks[0]].reshape(slab_size, emb_width)
    state_blocks = adagrad_state.reshape(row_count // BLOCK, BLOCK)
    state_row = state_blocks[touched_blocks[0]].reshape(1, slab_size)
    new_rows, state_next = fused_step(n, rows, weights, slab, state_row, dither[0])
    updated_blocks = table_blocks.at[touched_blocks[0]].set(
        new_rows.reshape(touch_count, BLOCK, emb_width)
    )
    updated_state = state_blocks.at[touched_blocks[0]].set(state_next.reshape(touch_count, BLOCK))
    return (updated_blocks.reshape(row_count, emb_width), updated_state.reshape(row_count))


def solution(mesh):
    return jax.shard_map(
        per_device,
        mesh=mesh,
        in_specs=(
            P(None, ("rep", "mp"), None, None),
            P(None, ("rep", "mp"), None, None),
            P(None, ("rep", "mp"), None, None),
            P("mp", None),
            P("mp"),
            P("mp", None),
            P("mp", None, None),
        ),
        out_specs=(P("mp", None), P("mp")),
        check_vma=False,
    )
```

```python
import functools

import jax
import jax.numpy as jnp
from jax import lax
from jax.experimental import pallas as pl
from jax.experimental.pallas import tpu as pltpu
from jax.sharding import PartitionSpec as P

BLOCK = 64
LEARN_RATE = 0.1
POOL_DECAY = 0.5
DITHER_UNIT = 2.0 ** (-15)
SMALLEST = 2.0 ** (-14)
KEEP_BYTES = 8 << 20
MESH = pl.DeviceIdType.MESH


def dither_round(weights, dither_bits):
    magnitude = jnp.maximum(jnp.abs(weights), SMALLEST)
    spacing = jnp.exp2(jnp.floor(jnp.log2(magnitude)) - 7.0)
    grid_level = jnp.floor(weights / spacing + dither_bits.astype(jnp.float32) * DITHER_UNIT)
    return (grid_level * spacing).astype(jnp.bfloat16)


def step_kernel(
    n,
    rows_ref,
    w_ref,
    slab_ref,
    state_ref,
    dither_ref,
    out_ref,
    state_out_ref,
    near,
    far,
    w_other,
    slab_t,
    pooled_out,
    pooled_in,
    grad_out,
    grad_in,
    kept,
    total,
    squares,
    rows_new,
    small_sem,
    rows_send,
    near_recv,
    far_recv,
    pooled_send,
    pooled_recv,
    grad_send,
    grad_recv,
):
    me = lax.axis_index("mp")
    rep = lax.axis_index("rep")
    m = n // 2
    group = me // m
    local = lax.rem(me, m)
    mirror = lax.rem(me + m, n)
    bags, samples = rows_ref.shape[2:]
    slab_size = slab_ref.shape[0]
    width = slab_t.shape[1]
    keeps = kept.shape[1] == m
    columns = pl.ds(pl.multiple_of(rep * width, width), width)

    def at(peer):
        return {"device_id": (rep, peer), "device_id_type": MESH}

    partner = {"device_id": (1 - rep, me), "device_id_type": MESH}

    def each(first, body):
        def run(step, carry):
            body(lax.rem(local + step, m))
            return carry

        lax.fori_loop(first, m, run, 0)

    def near_at(j):
        return group * m + j

    def far_at(j):
        return (1 - group) * m + j

    barrier = pltpu.get_barrier_semaphore()
    each(1, lambda j: pl.semaphore_signal(barrier, inc=1, **at(near_at(j))))
    each(0, lambda j: pl.semaphore_signal(barrier, inc=1, **at(far_at(j))))
    pl.semaphore_signal(barrier, inc=1, **partner)
    slab_t[0] = slab_ref[:, columns].astype(jnp.float32).T.astype(jnp.bfloat16)
    own_rows = pltpu.make_async_copy(rows_ref.at[local], near.at[rep, local], small_sem.at[0])
    own_rows.start()
    total[...] = jnp.zeros_like(total)
    pl.semaphore_wait(barrier, n)

    def near_copy(j, slot):
        return pltpu.make_async_remote_copy(
            rows_ref.at[j],
            near.at[rep, slot],
            rows_send.at[0, j],
            near_recv.at[slot],
            **at(near_at(j)),
        )

    def far_copy(j, slot):
        return pltpu.make_async_remote_copy(
            rows_ref.at[j, 1 - group],
            far.at[rep, slot],
            rows_send.at[1, j],
            far_recv.at[slot],
            **at(far_at(j)),
        )

    each(1, lambda j: near_copy(j, local).start())
    slab_copy = pltpu.make_async_remote_copy(
        slab_t.at[0], slab_t.at[1], small_sem.at[9], small_sem.at[10], **at(mirror)
    )
    slab_copy.start()
    w_copy = pltpu.make_async_remote_copy(
        w_ref, w_other, small_sem.at[1], small_sem.at[2], **partner
    )
    w_copy.start()
    each(0, lambda j: far_copy(j, local).start())
    own_rows.wait()
    each(1, lambda j: near_copy(j, j).wait_recv())
    swap_near = pltpu.make_async_remote_copy(
        near.at[rep], near.at[rep], small_sem.at[3], small_sem.at[4], **partner
    )
    swap_near.start()

    offset_in_block = lax.broadcasted_iota(jnp.int32, (BLOCK, samples), 0)
    offset_in_block = offset_in_block.astype(jnp.float32).astype(jnp.bfloat16)
    one = jnp.ones((BLOCK, samples), jnp.bfloat16)

    def hits(rows):
        blocks = []
        block_of, offset_of = rows // BLOCK, lax.rem(rows, BLOCK)
        for block in range(slab_size // BLOCK):
            wanted = jnp.where(block_of == block, offset_of, -1).astype(jnp.float32)
            counted = jnp.zeros((BLOCK, samples), jnp.bfloat16)
            for lookup in range(bags):
                row = jnp.broadcast_to(wanted[lookup : lookup + 1, :], (BLOCK, samples))
                same = row.astype(jnp.bfloat16) == offset_in_block
                counted = counted + jnp.where(same, one, jnp.zeros_like(one))
            blocks.append(counted)
        return jnp.concatenate(blocks, axis=0)

    def pooled_copy(part, which, j, slot):
        return pltpu.make_async_remote_copy(
            pooled_out.at[part, which, j],
            pooled_in.at[part, slot],
            pooled_send.at[part, which, j],
            pooled_recv.at[part, slot],
            **at(near_at(j)),
        )

    def grad_copy(part, peer, slot):
        return pltpu.make_async_remote_copy(
            grad_out.at[part, peer],
            grad_in.at[part, slot],
            grad_send.at[part, peer],
            grad_recv.at[part, slot],
            **at(peer),
        )

    def pool(part, replica, which):
        table = group if which == 0 else 1 - group
        feature = me if which == 0 else mirror

        def pooled(j):
            counted = hits(near[replica, j, table])
            if which == 0 and keeps:
                kept[part, j] = counted
            return jnp.dot(slab_t[which], counted, preferred_element_type=jnp.float32).astype(
                jnp.bfloat16
            )

        def send(j):
            pooled_out[part, which, j] = pooled(j)
            pooled_copy(part, which, j, feature).start()

        each(1, send)
        pooled_in[part, feature] = pooled(local)

    def interact(part, weights):
        def arrive(j):
            pooled_copy(part, 0, j, near_at(j)).wait_recv()
            pooled_copy(part, 1, j, far_at(j)).wait_recv()

        each(1, arrive)

        def mixed(feature):
            def add(other, carry):
                weight = weights[pl.ds(feature * n + other, 1), :]
                return carry + weight * pooled_in[part, other].astype(jnp.float32)

            zero = jnp.zeros((width, samples), jnp.float32)
            return lax.fori_loop(0, n, add, zero, unroll=4).astype(jnp.bfloat16)

        def send(peer):
            grad_out[part, peer] = mixed(peer)
            grad_copy(part, peer, me).start()

        each(0, lambda j: send(far_at(j)))
        each(1, lambda j: send(near_at(j)))
        grad_in[part, me] = mixed(me)

    def collect(part, replica):
        def add(peer, counted):
            total[...] += lax.dot_general(
                counted,
                grad_in[part, peer],
                (((1,), (1,)), ((), ())),
                preferred_element_type=jnp.float32,
            )

        def near_hits(j):
            return kept[part, j] if keeps else hits(near[replica, j, group])

        def take_near(j):
            grad_copy(part, near_at(j), near_at(j)).wait_recv()
            add(near_at(j), near_hits(j))

        def take_far(j):
            counted = hits(far[replica, j])
            grad_copy(part, far_at(j), far_at(j)).wait_recv()
            add(far_at(j), counted)

        add(me, near_hits(local))
        each(1, take_near)
        each(0, take_far)

    pool(0, rep, 0)
    swap_near.wait_recv()
    pool(1, 1 - rep, 0)
    each(0, lambda j: far_copy(j, j).wait_recv())
    swap_far = pltpu.make_async_remote_copy(
        far.at[rep], far.at[rep], small_sem.at[11], small_sem.at[12], **partner
    )
    swap_far.start()
    slab_copy.wait_recv()
    pool(0, rep, 1)
    pool(1, 1 - rep, 1)
    interact(0, w_ref)
    w_copy.wait_recv()
    interact(1, w_other)
    collect(0, rep)
    swap_far.wait_recv()
    collect(1, 1 - rep)

    grad = total[...]
    squares[0] = jnp.sum((grad * grad).T, axis=0, keepdims=True)
    square_copy = pltpu.make_async_remote_copy(
        squares.at[0], squares.at[1], small_sem.at[5], small_sem.at[6], **partner
    )
    square_copy.start()
    square_copy.wait_recv()
    first = jnp.where(rep == 0, squares[0], squares[1])
    second = jnp.where(rep == 0, squares[1], squares[0])
    state_next = state_ref[...] + (first + second) / (2.0 * width)
    state_out_ref[...] = state_next
    divisor = jnp.broadcast_to(jnp.sqrt(state_next) + 1e-08, (width, slab_size)).T
    moved = slab_ref[:, columns].astype(jnp.float32) - LEARN_RATE * grad / divisor
    rows_new[0] = dither_round(moved, dither_ref[:, columns])
    new_copy = pltpu.make_async_remote_copy(
        rows_new.at[0], rows_new.at[1], small_sem.at[7], small_sem.at[8], **partner
    )
    new_copy.start()
    out_ref[:, columns] = rows_new[0]

    each(1, lambda j: near_copy(j, j).wait_send())
    each(0, lambda j: far_copy(j, j).wait_send())
    for part in range(2):
        for which in range(2):
            each(1, lambda j: pooled_copy(part, which, j, j).wait_send())
        each(1, lambda j: grad_copy(part, near_at(j), me).wait_send())
        each(0, lambda j: grad_copy(part, far_at(j), me).wait_send())
    slab_copy.wait_send()
    w_copy.wait_send()
    swap_near.wait_send()
    swap_far.wait_send()
    square_copy.wait_send()
    new_copy.wait()
    out_ref[:, pl.ds(pl.multiple_of((1 - rep) * width, width), width)] = rows_new[1]


def fused_step(n, rows, weights, slab, state_row, dither):
    bags, samples = rows.shape[2:]
    slab_size, emb_width = slab.shape
    width = emb_width // 2
    m = n // 2
    keep = m if 4 * m * slab_size * samples <= KEEP_BYTES else 1
    dma = pltpu.SemaphoreType.DMA
    block = (2, n, width, samples)
    vmem = pl.BlockSpec(memory_space=pltpu.VMEM)
    return pl.pallas_call(
        functools.partial(step_kernel, n),
        out_shape=(
            jax.ShapeDtypeStruct((slab_size, emb_width), jnp.bfloat16),
            jax.ShapeDtypeStruct((1, slab_size), jnp.float32),
        ),
        in_specs=[vmem] * 5,
        out_specs=(vmem, vmem),
        scratch_shapes=[
            pltpu.VMEM((2, m, 2, bags, samples), jnp.int32),
            pltpu.VMEM((2, m, bags, samples), jnp.int32),
            pltpu.VMEM(weights.shape, jnp.float32),
            pltpu.VMEM((2, width, slab_size), jnp.bfloat16),
            pltpu.VMEM((2, 2, m, width, samples), jnp.bfloat16),
            pltpu.VMEM(block, jnp.bfloat16),
            pltpu.VMEM(block, jnp.bfloat16),
            pltpu.VMEM(block, jnp.bfloat16),
            pltpu.VMEM((2, keep, slab_size, samples), jnp.bfloat16),
            pltpu.VMEM((slab_size, width), jnp.float32),
            pltpu.VMEM((2, 1, slab_size), jnp.float32),
            pltpu.VMEM((2, slab_size, width), jnp.bfloat16),
            dma((13,)),
            dma((2, m)),
            dma((m,)),
            dma((m,)),
            dma((2, 2, m)),
            dma((2, n)),
            dma((2, n)),
            dma((2, n)),
        ],
        compiler_params=pltpu.CompilerParams(collective_id=0, has_side_effects=True),
        name="fused_step",
    )(rows, weights, slab, state_row, dither)


def per_device(
    lookup_block, lookup_offset, interaction_grad, table, adagrad_state, touched_blocks, dither
):
    micro_count, sample_count, feature_count, bag_count = lookup_block.shape
    n = lax.axis_size("mp")
    samples = micro_count * sample_count
    row_count, emb_width = table.shape
    touch_count = touched_blocks.shape[1]
    slab_size = touch_count * BLOCK
    rows = (lookup_block * BLOCK + lookup_offset).reshape(samples, feature_count * bag_count)
    rows = rows.T.reshape(2, feature_count // 2, bag_count, samples).swapaxes(0, 1)
    cot = interaction_grad.reshape(samples, feature_count, feature_count).astype(jnp.float32)
    weights = cot + jnp.swapaxes(cot, 1, 2) + POOL_DECAY * jnp.eye(feature_count)
    weights = weights.reshape(samples, feature_count * feature_count).T
    table_blocks = table.reshape(row_count // BLOCK, BLOCK, emb_width)
    slab = table_blocks[touched_blocks[0]].reshape(slab_size, emb_width)
    state_blocks = adagrad_state.reshape(row_count // BLOCK, BLOCK)
    state_row = state_blocks[touched_blocks[0]].reshape(1, slab_size)
    new_rows, state_next = fused_step(n, rows, weights, slab, state_row, dither[0])
    updated_blocks = table_blocks.at[touched_blocks[0]].set(
        new_rows.reshape(touch_count, BLOCK, emb_width)
    )
    updated_state = state_blocks.at[touched_blocks[0]].set(state_next.reshape(touch_count, BLOCK))
    return (updated_blocks.reshape(row_count, emb_width), updated_state.reshape(row_count))


def solution(mesh):
    return jax.shard_map(
        per_device,
        mesh=mesh,
        in_specs=(
            P(None, ("rep", "mp"), None, None),
            P(None, ("rep", "mp"), None, None),
            P(None, ("rep", "mp"), None, None),
            P("mp", None),
            P("mp"),
            P("mp", None),
            P("mp", None, None),
        ),
        out_specs=(P("mp", None), P("mp")),
        check_vma=False,
    )
```

```python
import functools
import math

import jax
import jax.numpy as jnp
from jax import lax
from jax.experimental import pallas as pl
from jax.experimental.pallas import tpu as pltpu
from jax.sharding import PartitionSpec as P

BLOCK = 64
LEARN_RATE = 0.1
POOL_DECAY = 0.5
DITHER_UNIT = 2.0 ** (-15)
SMALLEST = 2.0 ** (-14)
KEEP_BYTES = 8 << 20
MESH = pl.DeviceIdType.MESH


def dither_round(weights, dither_bits):
    magnitude = jnp.maximum(jnp.abs(weights), SMALLEST)
    spacing = jnp.exp2(jnp.floor(jnp.log2(magnitude)) - 7.0)
    grid_level = jnp.floor(weights / spacing + dither_bits.astype(jnp.float32) * DITHER_UNIT)
    return (grid_level * spacing).astype(jnp.bfloat16)


def step_kernel(
    n,
    rows_ref,
    w_ref,
    touched_ref,
    state_ref,
    table_ref,
    dither_ref,
    out_ref,
    state_out_ref,
    near,
    far,
    w_other,
    table_in,
    dither_in,
    slab,
    slab_t,
    pooled_out,
    pooled_in,
    grad_out,
    grad_in,
    kept,
    total,
    squares,
    rows_new,
    small_sem,
    rows_send,
    near_recv,
    far_recv,
    pooled_send,
    pooled_recv,
    grad_send,
    grad_recv,
):
    me = lax.axis_index("mp")
    rep = lax.axis_index("rep")
    m = n // 2
    group = me // m
    local = lax.rem(me, m)
    mirror = lax.rem(me + m, n)
    samples = w_ref.shape[1]
    bags = rows_ref.shape[3]
    slab_size, width = slab.shape
    touch_count = slab_size // BLOCK
    keeps = kept.shape[1] == m
    columns = pl.ds(pl.multiple_of(rep * width, width), width)

    def at(peer):
        return {"device_id": (rep, peer), "device_id_type": MESH}

    partner = {"device_id": (1 - rep, me), "device_id_type": MESH}

    def each(first, body):
        def run(step, carry):
            body(lax.rem(local + step, m))
            return carry

        lax.fori_loop(first, m, run, 0)

    def near_at(j):
        return group * m + j

    def far_at(j):
        return (1 - group) * m + j

    table_copy = pltpu.make_async_copy(table_ref.at[:, :, columns], table_in, small_sem.at[13])
    table_copy.start()
    own_rows = pltpu.make_async_copy(
        rows_ref.at[:, :, local], near.at[rep, local], small_sem.at[0]
    )
    own_rows.start()
    dither_copy = pltpu.make_async_copy(dither_ref.at[:, columns], dither_in, small_sem.at[14])
    dither_copy.start()
    barrier = pltpu.get_barrier_semaphore()
    each(1, lambda j: pl.semaphore_signal(barrier, inc=1, **at(near_at(j))))
    each(0, lambda j: pl.semaphore_signal(barrier, inc=1, **at(far_at(j))))
    pl.semaphore_signal(barrier, inc=1, **partner)
    total[...] = jnp.zeros_like(total)
    table_copy.wait()
    for block in range(touch_count):
        slab[block * BLOCK : (block + 1) * BLOCK, :] = table_in[touched_ref[0, block]]
    slab_t[0] = slab[...].astype(jnp.float32).T.astype(jnp.bfloat16)
    pl.semaphore_wait(barrier, n)

    def near_copy(j, slot):
        return pltpu.make_async_remote_copy(
            rows_ref.at[:, :, j],
            near.at[rep, slot],
            rows_send.at[0, j],
            near_recv.at[slot],
            **at(near_at(j)),
        )

    def far_copy(j, slot):
        return pltpu.make_async_remote_copy(
            rows_ref.at[:, 1 - group, j],
            far.at[rep, slot],
            rows_send.at[1, j],
            far_recv.at[slot],
            **at(far_at(j)),
        )

    each(1, lambda j: near_copy(j, local).start())
    slab_copy = pltpu.make_async_remote_copy(
        slab_t.at[0], slab_t.at[1], small_sem.at[9], small_sem.at[10], **at(mirror)
    )
    slab_copy.start()
    w_copy = pltpu.make_async_remote_copy(
        w_ref, w_other, small_sem.at[1], small_sem.at[2], **partner
    )
    w_copy.start()
    each(0, lambda j: far_copy(j, local).start())
    own_rows.wait()
    each(1, lambda j: near_copy(j, j).wait_recv())
    swap_near = pltpu.make_async_remote_copy(
        near.at[rep], near.at[rep], small_sem.at[3], small_sem.at[4], **partner
    )
    swap_near.start()

    offset_in_block = lax.broadcasted_iota(jnp.int32, (BLOCK, samples), 0)
    offset_in_block = offset_in_block.astype(jnp.float32).astype(jnp.bfloat16)
    one = jnp.ones((BLOCK, samples), jnp.bfloat16)

    def hits(micros):
        rows = jnp.concatenate([micros[i] for i in range(micros.shape[0])], axis=-1)
        blocks = []
        block_of, offset_of = rows // BLOCK, lax.rem(rows, BLOCK)
        for block in range(slab_size // BLOCK):
            wanted = jnp.where(block_of == block, offset_of, -1).astype(jnp.float32)
            counted = jnp.zeros((BLOCK, samples), jnp.bfloat16)
            for lookup in range(bags):
                row = jnp.broadcast_to(wanted[lookup : lookup + 1, :], (BLOCK, samples))
                same = row.astype(jnp.bfloat16) == offset_in_block
                counted = counted + jnp.where(same, one, jnp.zeros_like(one))
            blocks.append(counted)
        return jnp.concatenate(blocks, axis=0)

    def pooled_copy(part, which, j, slot):
        return pltpu.make_async_remote_copy(
            pooled_out.at[part, which, j],
            pooled_in.at[part, slot],
            pooled_send.at[part, which, j],
            pooled_recv.at[part, slot],
            **at(near_at(j)),
        )

    def grad_copy(part, peer, slot):
        return pltpu.make_async_remote_copy(
            grad_out.at[part, peer],
            grad_in.at[part, slot],
            grad_send.at[part, peer],
            grad_recv.at[part, slot],
            **at(peer),
        )

    def pool(part, replica, which):
        table = group if which == 0 else 1 - group
        feature = me if which == 0 else mirror

        def pooled(j):
            counted = hits(near[replica, j, :, table])
            if which == 0 and keeps:
                kept[part, j] = counted
            return jnp.dot(slab_t[which], counted, preferred_element_type=jnp.float32).astype(
                jnp.bfloat16
            )

        def send(j):
            pooled_out[part, which, j] = pooled(j)
            pooled_copy(part, which, j, feature).start()

        each(1, send)
        pooled_in[part, feature] = pooled(local)

    def interact(part, weights):
        def arrive(j):
            pooled_copy(part, 0, j, near_at(j)).wait_recv()
            pooled_copy(part, 1, j, far_at(j)).wait_recv()

        each(1, arrive)

        def mixed(feature):
            def add(other, carry):
                weight = (
                    weights[pl.ds(feature * n + other, 1), :]
                    + weights[pl.ds(other * n + feature, 1), :]
                )
                return carry + weight * pooled_in[part, other].astype(jnp.float32)

            start = POOL_DECAY * pooled_in[part, feature].astype(jnp.float32)
            return lax.fori_loop(0, n, add, start, unroll=4).astype(jnp.bfloat16)

        def send(peer):
            grad_out[part, peer] = mixed(peer)
            grad_copy(part, peer, me).start()

        each(0, lambda j: send(far_at(j)))
        each(1, lambda j: send(near_at(j)))
        grad_in[part, me] = mixed(me)

    def collect(part, replica):
        def add(peer, counted):
            total[...] += lax.dot_general(
                counted,
                grad_in[part, peer],
                (((1,), (1,)), ((), ())),
                preferred_element_type=jnp.float32,
            )

        def near_hits(j):
            return kept[part, j] if keeps else hits(near[replica, j, :, group])

        def take_near(j):
            grad_copy(part, near_at(j), near_at(j)).wait_recv()
            add(near_at(j), near_hits(j))

        def take_far(j):
            counted = hits(far[replica, j])
            grad_copy(part, far_at(j), far_at(j)).wait_recv()
            add(far_at(j), counted)

        add(me, near_hits(local))
        each(1, take_near)
        each(0, take_far)

    pool(0, rep, 0)
    swap_near.wait_recv()
    pool(1, 1 - rep, 0)
    each(0, lambda j: far_copy(j, j).wait_recv())
    swap_far = pltpu.make_async_remote_copy(
        far.at[rep], far.at[rep], small_sem.at[11], small_sem.at[12], **partner
    )
    swap_far.start()
    slab_copy.wait_recv()
    pool(0, rep, 1)
    pool(1, 1 - rep, 1)
    interact(0, w_ref)
    w_copy.wait_recv()
    interact(1, w_other)
    collect(0, rep)
    swap_far.wait_recv()
    collect(1, 1 - rep)

    pieces = []
    for block in range(touch_count):
        at_block = touched_ref[0, block]
        pair = state_ref[pl.ds(at_block // 2, 1), :]
        pieces.append(jnp.where(lax.rem(at_block, 2) == 0, pair[:, :BLOCK], pair[:, BLOCK:]))
    state_row = jnp.concatenate(pieces, axis=1)
    grad = total[...]
    squares[0] = jnp.sum((grad * grad).T, axis=0, keepdims=True)
    square_copy = pltpu.make_async_remote_copy(
        squares.at[0], squares.at[1], small_sem.at[5], small_sem.at[6], **partner
    )
    square_copy.start()
    square_copy.wait_recv()
    first = jnp.where(rep == 0, squares[0], squares[1])
    second = jnp.where(rep == 0, squares[1], squares[0])
    state_next = state_row + (first + second) / (2.0 * width)
    divisor = jnp.broadcast_to(jnp.sqrt(state_next) + 1e-08, (width, slab_size)).T
    moved = slab[...].astype(jnp.float32) - LEARN_RATE * grad / divisor
    dither_copy.wait()
    rows_new[0] = dither_round(moved, dither_in[...])
    new_copy = pltpu.make_async_remote_copy(
        rows_new.at[0], rows_new.at[1], small_sem.at[7], small_sem.at[8], **partner
    )
    new_copy.start()
    out_ref[:, columns] = rows_new[0]
    state_all = state_ref[...]
    block_at = 2 * lax.broadcasted_iota(jnp.int32, state_all.shape, 0)
    block_at = block_at + lax.broadcasted_iota(jnp.int32, state_all.shape, 1) // BLOCK
    for block in range(touch_count):
        piece = state_next[:, block * BLOCK : (block + 1) * BLOCK]
        piece = jnp.broadcast_to(jnp.concatenate([piece, piece], axis=1), state_all.shape)
        state_all = jnp.where(block_at == touched_ref[0, block], piece, state_all)
    state_out_ref[...] = state_all

    each(1, lambda j: near_copy(j, j).wait_send())
    each(0, lambda j: far_copy(j, j).wait_send())
    for part in range(2):
        for which in range(2):
            each(1, lambda j: pooled_copy(part, which, j, j).wait_send())
        each(1, lambda j: grad_copy(part, near_at(j), me).wait_send())
        each(0, lambda j: grad_copy(part, far_at(j), me).wait_send())
    slab_copy.wait_send()
    w_copy.wait_send()
    swap_near.wait_send()
    swap_far.wait_send()
    square_copy.wait_send()
    new_copy.wait()
    out_ref[:, pl.ds(pl.multiple_of((1 - rep) * width, width), width)] = rows_new[1]


def fused_step(n, rows, weights, touched, state, table, dither):
    micros, _, _, bags, _ = rows.shape
    samples = weights.shape[1]
    slab_size, emb_width = dither.shape
    width = emb_width // 2
    m = n // 2
    keep = m if 4 * m * slab_size * samples <= KEEP_BYTES else 1
    dma = pltpu.SemaphoreType.DMA
    block = (2, n, width, samples)
    vmem = pl.BlockSpec(memory_space=pltpu.VMEM)
    smem = pl.BlockSpec(memory_space=pltpu.SMEM)
    hbm = pl.BlockSpec(memory_space=pl.ANY)
    return pl.pallas_call(
        functools.partial(step_kernel, n),
        out_shape=(
            jax.ShapeDtypeStruct((slab_size, emb_width), jnp.bfloat16),
            jax.ShapeDtypeStruct(state.shape, jnp.float32),
        ),
        in_specs=[vmem, vmem, smem, vmem, hbm, hbm],
        out_specs=(vmem, vmem),
        scratch_shapes=[
            pltpu.VMEM((2, m, micros, 2) + rows.shape[3:], jnp.int32),
            pltpu.VMEM((2, m, micros) + rows.shape[3:], jnp.int32),
            pltpu.VMEM(weights.shape, jnp.float32),
            pltpu.VMEM(table.shape[:2] + (width,), jnp.bfloat16),
            pltpu.VMEM((slab_size, width), jnp.int32),
            pltpu.VMEM((slab_size, width), jnp.bfloat16),
            pltpu.VMEM((2, width, slab_size), jnp.bfloat16),
            pltpu.VMEM((2, 2, m, width, samples), jnp.bfloat16),
            pltpu.VMEM(block, jnp.bfloat16),
            pltpu.VMEM(block, jnp.bfloat16),
            pltpu.VMEM(block, jnp.bfloat16),
            pltpu.VMEM((2, keep, slab_size, samples), jnp.bfloat16),
            pltpu.VMEM((slab_size, width), jnp.float32),
            pltpu.VMEM((2, 1, slab_size), jnp.float32),
            pltpu.VMEM((2, slab_size, width), jnp.bfloat16),
            dma((15,)),
            dma((2, m)),
            dma((m,)),
            dma((m,)),
            dma((2, 2, m)),
            dma((2, n)),
            dma((2, n)),
            dma((2, n)),
        ],
        compiler_params=pltpu.CompilerParams(collective_id=0, has_side_effects=True),
        name="fused_step",
    )(rows, weights, touched, state, table, dither)


def write_kernel(chunks, touched_ref, new_ref, table_ref, out_ref, held, read_sem, write_sem):
    size = table_ref.shape[0] // chunks

    def read(chunk):
        part = pl.ds(chunk * size, size)
        return pltpu.make_async_copy(table_ref.at[part], held.at[part], read_sem.at[chunk])

    def write(chunk):
        part = pl.ds(chunk * size, size)
        return pltpu.make_async_copy(held.at[part], out_ref.at[part], write_sem.at[chunk])

    for chunk in range(chunks):
        read(chunk).start()
    for chunk in range(chunks):
        read(chunk).wait()
        for block in range(touched_ref.shape[1]):
            target = touched_ref[0, block]

            @pl.when((target >= chunk * size) & (target < (chunk + 1) * size))
            def _():
                held[target] = new_ref[block]

        write(chunk).start()
    for chunk in range(chunks):
        write(chunk).wait()


def write_table(touched, new_rows, table):
    chunks = math.gcd(table.shape[0], 4)
    hbm = pl.BlockSpec(memory_space=pl.ANY)
    return pl.pallas_call(
        functools.partial(write_kernel, chunks),
        out_shape=jax.ShapeDtypeStruct(table.shape, table.dtype),
        in_specs=[
            pl.BlockSpec(memory_space=pltpu.SMEM),
            pl.BlockSpec(memory_space=pltpu.VMEM),
            hbm,
        ],
        out_specs=hbm,
        scratch_shapes=[
            pltpu.VMEM(table.shape, table.dtype),
            pltpu.SemaphoreType.DMA((chunks,)),
            pltpu.SemaphoreType.DMA((chunks,)),
        ],
        name="write_table",
    )(touched, new_rows, table)


def per_device(
    lookup_block, lookup_offset, interaction_grad, table, adagrad_state, touched_blocks, dither
):
    micro_count, sample_count, feature_count, bag_count = lookup_block.shape
    n = lax.axis_size("mp")
    row_count, emb_width = table.shape
    touch_count = touched_blocks.shape[1]
    rows = (lookup_block * BLOCK + lookup_offset).transpose(0, 2, 3, 1)
    rows = rows.reshape(micro_count, 2, feature_count // 2, bag_count, sample_count)
    cot = interaction_grad.transpose(2, 3, 0, 1).astype(jnp.float32)
    cot = cot.reshape(feature_count * feature_count, micro_count * sample_count)
    table_blocks = table.reshape(row_count // BLOCK, BLOCK, emb_width)
    state = adagrad_state.reshape(row_count // (2 * BLOCK), 2 * BLOCK)
    new_rows, new_state = fused_step(
        n, rows, cot, touched_blocks, state, table_blocks, dither[0]
    )
    new_table = write_table(
        touched_blocks, new_rows.reshape(touch_count, BLOCK, emb_width), table_blocks
    )
    return (new_table.reshape(row_count, emb_width), new_state.reshape(row_count))


def solution(mesh):
    return jax.shard_map(
        per_device,
        mesh=mesh,
        in_specs=(
            P(None, ("rep", "mp"), None, None),
            P(None, ("rep", "mp"), None, None),
            P(None, ("rep", "mp"), None, None),
            P("mp", None),
            P("mp"),
            P("mp", None),
            P("mp", None, None),
        ),
        out_specs=(P("mp", None), P("mp")),
        check_vma=False,
    )
```

```python
import functools
import math

import jax
import jax.numpy as jnp
from jax import lax
from jax.experimental import pallas as pl
from jax.experimental.pallas import tpu as pltpu
from jax.sharding import PartitionSpec as P

BLOCK = 64
LEARN_RATE = 0.1
POOL_DECAY = 0.5
DITHER_UNIT = 2.0 ** (-15)
SMALLEST = 2.0 ** (-14)
KEEP_BYTES = 8 << 20
MESH = pl.DeviceIdType.MESH


def dither_round(weights, dither_bits):
    magnitude = jnp.maximum(jnp.abs(weights), SMALLEST)
    spacing = jnp.exp2(jnp.floor(jnp.log2(magnitude)) - 7.0)
    grid_level = jnp.floor(weights / spacing + dither_bits.astype(jnp.float32) * DITHER_UNIT)
    return (grid_level * spacing).astype(jnp.bfloat16)


def step_kernel(
    n,
    block_hbm,
    offset_hbm,
    cot_ref,
    touched_ref,
    state_hbm,
    table_ref,
    dither_ref,
    out_ref,
    state_out_ref,
    block_ref,
    offset_ref,
    state_ref,
    rows_ref,
    cot_in,
    near,
    far,
    w_ref,
    w_other,
    table_in,
    dither_in,
    slab,
    slab_t,
    pooled_out,
    pooled_in,
    grad_out,
    grad_in,
    kept,
    total,
    squares,
    rows_new,
    small_sem,
    rows_send,
    near_recv,
    far_recv,
    pooled_send,
    pooled_recv,
    grad_send,
    grad_recv,
):
    me = lax.axis_index("mp")
    rep = lax.axis_index("rep")
    m = n // 2
    group = me // m
    local = lax.rem(me, m)
    mirror = lax.rem(me + m, n)
    samples = w_ref.shape[1]
    bags = rows_ref.shape[3]
    slab_size, width = slab.shape
    touch_count = slab_size // BLOCK
    keeps = kept.shape[1] == m
    columns = pl.ds(pl.multiple_of(rep * width, width), width)

    def at(peer):
        return {"device_id": (rep, peer), "device_id_type": MESH}

    partner = {"device_id": (1 - rep, me), "device_id_type": MESH}

    def each(first, body):
        def run(step, carry):
            body(lax.rem(local + step, m))
            return carry

        lax.fori_loop(first, m, run, 0)

    def near_at(j):
        return group * m + j

    def far_at(j):
        return (1 - group) * m + j

    barrier = pltpu.get_barrier_semaphore()
    each(1, lambda j: pl.semaphore_signal(barrier, inc=1, **at(near_at(j))))
    each(0, lambda j: pl.semaphore_signal(barrier, inc=1, **at(far_at(j))))
    pl.semaphore_signal(barrier, inc=1, **partner)
    block_copy = pltpu.make_async_copy(block_hbm, block_ref, small_sem.at[17])
    block_copy.start()
    offset_copy = pltpu.make_async_copy(offset_hbm, offset_ref, small_sem.at[18])
    offset_copy.start()
    state_copy = pltpu.make_async_copy(state_hbm, state_ref, small_sem.at[19])
    state_copy.start()
    table_copy = pltpu.make_async_copy(table_ref.at[:, :, columns], table_in, small_sem.at[13])
    table_copy.start()
    dither_copy = pltpu.make_async_copy(dither_ref.at[:, columns], dither_in, small_sem.at[14])
    dither_copy.start()
    block_copy.wait()
    offset_copy.wait()
    rows_ref[...] = block_ref[...] * BLOCK + offset_ref[...]
    near[rep, local] = rows_ref[:, :, local]
    total[...] = jnp.zeros_like(total)
    table_copy.wait()
    for block in range(touch_count):
        slab[block * BLOCK : (block + 1) * BLOCK, :] = table_in[touched_ref[0, block]]
    slab_t[0] = slab[...].astype(jnp.float32).T.astype(jnp.bfloat16)
    pl.semaphore_wait(barrier, n)

    def near_copy(j, slot):
        return pltpu.make_async_remote_copy(
            rows_ref.at[:, :, j],
            near.at[rep, slot],
            rows_send.at[0, j],
            near_recv.at[slot],
            **at(near_at(j)),
        )

    def far_copy(j, slot):
        return pltpu.make_async_remote_copy(
            rows_ref.at[:, 1 - group, j],
            far.at[rep, slot],
            rows_send.at[1, j],
            far_recv.at[slot],
            **at(far_at(j)),
        )

    each(1, lambda j: near_copy(j, local).start())
    slab_copy = pltpu.make_async_remote_copy(
        slab_t.at[0], slab_t.at[1], small_sem.at[9], small_sem.at[10], **at(mirror)
    )
    slab_copy.start()
    each(0, lambda j: far_copy(j, local).start())
    cot_size = cot_in.shape[1]

    def spread(chunk, carry):
        cot_copy = pltpu.make_async_copy(
            cot_ref.at[:, pl.ds(chunk * cot_size, cot_size)], cot_in, small_sem.at[0]
        )
        cot_copy.start()
        cot_copy.wait()
        for i in range(cot_size):
            pieces = [cot_in[micro, i].astype(jnp.float32) for micro in range(cot_in.shape[0])]
            at_row = pl.multiple_of((chunk * cot_size + i) * n, n)
            w_ref[pl.ds(at_row, n), :] = jnp.concatenate(pieces, axis=-1)
        return carry

    lax.fori_loop(0, n // cot_size, spread, 0)
    w_copy = pltpu.make_async_remote_copy(
        w_ref, w_other, small_sem.at[1], small_sem.at[2], **partner
    )
    w_copy.start()
    each(1, lambda j: near_copy(j, j).wait_recv())
    swap_near = pltpu.make_async_remote_copy(
        near.at[rep], near.at[rep], small_sem.at[3], small_sem.at[4], **partner
    )
    swap_near.start()

    offset_in_block = lax.broadcasted_iota(jnp.int32, (BLOCK, samples), 0)
    offset_in_block = offset_in_block.astype(jnp.float32).astype(jnp.bfloat16)
    one = jnp.ones((BLOCK, samples), jnp.bfloat16)

    def hits(micros):
        rows = jnp.concatenate([micros[i] for i in range(micros.shape[0])], axis=-1)
        blocks = []
        block_of, offset_of = rows // BLOCK, lax.rem(rows, BLOCK)
        for block in range(slab_size // BLOCK):
            wanted = jnp.where(block_of == block, offset_of, -1).astype(jnp.float32)
            counted = jnp.zeros((BLOCK, samples), jnp.bfloat16)
            for lookup in range(bags):
                row = jnp.broadcast_to(wanted[lookup : lookup + 1, :], (BLOCK, samples))
                same = row.astype(jnp.bfloat16) == offset_in_block
                counted = counted + jnp.where(same, one, jnp.zeros_like(one))
            blocks.append(counted)
        return jnp.concatenate(blocks, axis=0)

    def pooled_copy(part, which, j, slot):
        return pltpu.make_async_remote_copy(
            pooled_out.at[part, which, j],
            pooled_in.at[part, slot],
            pooled_send.at[part, which, j],
            pooled_recv.at[part, slot],
            **at(near_at(j)),
        )

    def grad_copy(part, peer, slot):
        return pltpu.make_async_remote_copy(
            grad_out.at[part, peer],
            grad_in.at[part, slot],
            grad_send.at[part, peer],
            grad_recv.at[part, slot],
            **at(peer),
        )

    def pool(part, replica, which):
        table = group if which == 0 else 1 - group
        feature = me if which == 0 else mirror

        def pooled(j):
            counted = hits(near[replica, j, :, table])
            if which == 0 and keeps:
                kept[part, j] = counted
            return jnp.dot(slab_t[which], counted, preferred_element_type=jnp.float32).astype(
                jnp.bfloat16
            )

        def send(j):
            pooled_out[part, which, j] = pooled(j)
            pooled_copy(part, which, j, feature).start()

        each(1, send)
        pooled_in[part, feature] = pooled(local)

    def interact(part, weights):
        def arrive(j):
            pooled_copy(part, 0, j, near_at(j)).wait_recv()
            pooled_copy(part, 1, j, far_at(j)).wait_recv()

        each(1, arrive)

        def mixed(feature):
            def add(other, carry):
                weight = (
                    weights[pl.ds(feature * n + other, 1), :]
                    + weights[pl.ds(other * n + feature, 1), :]
                )
                return carry + weight * pooled_in[part, other].astype(jnp.float32)

            start = POOL_DECAY * pooled_in[part, feature].astype(jnp.float32)
            return lax.fori_loop(0, n, add, start, unroll=4).astype(jnp.bfloat16)

        def send(peer):
            grad_out[part, peer] = mixed(peer)
            grad_copy(part, peer, me).start()

        each(0, lambda j: send(far_at(j)))
        each(1, lambda j: send(near_at(j)))
        grad_in[part, me] = mixed(me)

    def collect(part, replica):
        def add(peer, counted):
            total[...] += lax.dot_general(
                counted,
                grad_in[part, peer],
                (((1,), (1,)), ((), ())),
                preferred_element_type=jnp.float32,
            )

        def near_hits(j):
            return kept[part, j] if keeps else hits(near[replica, j, :, group])

        def take_near(j):
            grad_copy(part, near_at(j), near_at(j)).wait_recv()
            add(near_at(j), near_hits(j))

        def take_far(j):
            counted = hits(far[replica, j])
            grad_copy(part, far_at(j), far_at(j)).wait_recv()
            add(far_at(j), counted)

        add(me, near_hits(local))
        each(1, take_near)
        each(0, take_far)

    pool(0, rep, 0)
    swap_near.wait_recv()
    pool(1, 1 - rep, 0)
    each(0, lambda j: far_copy(j, j).wait_recv())
    swap_far = pltpu.make_async_remote_copy(
        far.at[rep], far.at[rep], small_sem.at[11], small_sem.at[12], **partner
    )
    swap_far.start()
    slab_copy.wait_recv()
    pool(0, rep, 1)
    pool(1, 1 - rep, 1)
    interact(0, w_ref)
    w_copy.wait_recv()
    interact(1, w_other)
    collect(0, rep)
    swap_far.wait_recv()
    collect(1, 1 - rep)

    state_copy.wait()
    pieces = []
    for block in range(touch_count):
        at_block = touched_ref[0, block]
        pair = state_ref[pl.ds(at_block // 2, 1), :]
        pieces.append(jnp.where(lax.rem(at_block, 2) == 0, pair[:, :BLOCK], pair[:, BLOCK:]))
    state_row = jnp.concatenate(pieces, axis=1)
    grad = total[...]
    squares[0] = jnp.sum((grad * grad).T, axis=0, keepdims=True)
    square_copy = pltpu.make_async_remote_copy(
        squares.at[0], squares.at[1], small_sem.at[5], small_sem.at[6], **partner
    )
    square_copy.start()
    square_copy.wait_recv()
    first = jnp.where(rep == 0, squares[0], squares[1])
    second = jnp.where(rep == 0, squares[1], squares[0])
    state_next = state_row + (first + second) / (2.0 * width)
    divisor = jnp.broadcast_to(jnp.sqrt(state_next) + 1e-08, (width, slab_size)).T
    dither_copy.wait()
    size = slab_size // 2
    new_copies = []
    for piece in range(2):
        part = pl.ds(piece * size, size)
        span = slice(piece * size, (piece + 1) * size)
        moved = slab[span, :].astype(jnp.float32) - LEARN_RATE * total[span, :] / divisor[span]
        rows_new[0, span] = dither_round(moved, dither_in[span, :])
        new_copy = pltpu.make_async_remote_copy(
            rows_new.at[0, part],
            rows_new.at[1, part],
            small_sem.at[7 + 8 * piece],
            small_sem.at[8 + 8 * piece],
            **partner,
        )
        new_copy.start()
        new_copies.append(new_copy)
    out_ref[:, columns] = rows_new[0]
    state_all = state_ref[...]
    block_at = 2 * lax.broadcasted_iota(jnp.int32, state_all.shape, 0)
    block_at = block_at + lax.broadcasted_iota(jnp.int32, state_all.shape, 1) // BLOCK
    for block in range(touch_count):
        piece = state_next[:, block * BLOCK : (block + 1) * BLOCK]
        piece = jnp.broadcast_to(jnp.concatenate([piece, piece], axis=1), state_all.shape)
        state_all = jnp.where(block_at == touched_ref[0, block], piece, state_all)
    state_out_ref[...] = state_all

    each(1, lambda j: near_copy(j, j).wait_send())
    each(0, lambda j: far_copy(j, j).wait_send())
    for part in range(2):
        for which in range(2):
            each(1, lambda j: pooled_copy(part, which, j, j).wait_send())
        each(1, lambda j: grad_copy(part, near_at(j), me).wait_send())
        each(0, lambda j: grad_copy(part, far_at(j), me).wait_send())
    slab_copy.wait_send()
    w_copy.wait_send()
    swap_near.wait_send()
    swap_far.wait_send()
    square_copy.wait_send()
    for new_copy in new_copies:
        new_copy.wait()
    out_ref[:, pl.ds(pl.multiple_of((1 - rep) * width, width), width)] = rows_new[1]


def fused_step(n, blocks, offsets, cot, touched, state, table, dither):
    micros, sample_count = blocks.shape[0], blocks.shape[-1]
    samples = micros * sample_count
    cot_size = math.gcd(n, 16)
    slab_size, emb_width = dither.shape
    width = emb_width // 2
    m = n // 2
    keep = m if 4 * m * slab_size * samples <= KEEP_BYTES else 1
    dma = pltpu.SemaphoreType.DMA
    block = (2, n, width, samples)
    vmem = pl.BlockSpec(memory_space=pltpu.VMEM)
    smem = pl.BlockSpec(memory_space=pltpu.SMEM)
    hbm = pl.BlockSpec(memory_space=pltpu.HBM)
    return pl.pallas_call(
        functools.partial(step_kernel, n),
        out_shape=(
            jax.ShapeDtypeStruct((slab_size, emb_width), jnp.bfloat16),
            jax.ShapeDtypeStruct(state.shape, jnp.float32),
        ),
        in_specs=[hbm, hbm, hbm, smem, hbm, hbm, hbm],
        out_specs=(vmem, vmem),
        scratch_shapes=[
            pltpu.VMEM(blocks.shape, jnp.int32),
            pltpu.VMEM(blocks.shape, jnp.int32),
            pltpu.VMEM(state.shape, jnp.float32),
            pltpu.VMEM(blocks.shape, jnp.int32),
            pltpu.VMEM((micros, cot_size, n, sample_count), jnp.bfloat16),
            pltpu.VMEM((2, m, micros, 2) + blocks.shape[3:], jnp.int32),
            pltpu.VMEM((2, m, micros) + blocks.shape[3:], jnp.int32),
            pltpu.VMEM((n * n, samples), jnp.float32),
            pltpu.VMEM((n * n, samples), jnp.float32),
            pltpu.VMEM(table.shape[:2] + (width,), jnp.bfloat16),
            pltpu.VMEM((slab_size, width), jnp.int32),
            pltpu.VMEM((slab_size, width), jnp.bfloat16),
            pltpu.VMEM((2, width, slab_size), jnp.bfloat16),
            pltpu.VMEM((2, 2, m, width, samples), jnp.bfloat16),
            pltpu.VMEM(block, jnp.bfloat16),
            pltpu.VMEM(block, jnp.bfloat16),
            pltpu.VMEM(block, jnp.bfloat16),
            pltpu.VMEM((2, keep, slab_size, samples), jnp.bfloat16),
            pltpu.VMEM((slab_size, width), jnp.float32),
            pltpu.VMEM((2, 1, slab_size), jnp.float32),
            pltpu.VMEM((2, slab_size, width), jnp.bfloat16),
            dma((20,)),
            dma((2, m)),
            dma((m,)),
            dma((m,)),
            dma((2, 2, m)),
            dma((2, n)),
            dma((2, n)),
            dma((2, n)),
        ],
        compiler_params=pltpu.CompilerParams(collective_id=0, has_side_effects=True),
        name="fused_step",
    )(blocks, offsets, cot, touched, state, table, dither)


def write_kernel(touched_ref, new_ref, state_ref, table_ref, out_ref, state_out_ref, sem):
    state_out_ref[...] = state_ref[...]

    def write(block, carry):
        new = -1
        for i in range(touched_ref.shape[1]):
            new = jnp.where(touched_ref[0, i] == block, i, new)

        @pl.when(new >= 0)
        def _():
            pltpu.make_async_copy(new_ref.at[new], out_ref.at[block], sem).start()

        @pl.when(new < 0)
        def _():
            pltpu.make_async_copy(table_ref.at[block], out_ref.at[block], sem).start()

        return carry

    lax.fori_loop(0, table_ref.shape[0], write, 0)
    pltpu.make_async_copy(table_ref, out_ref, sem).wait()


def write_table(touched, new_rows, state, table):
    vmem = pl.BlockSpec(memory_space=pltpu.VMEM)
    return pl.pallas_call(
        write_kernel,
        out_shape=(
            jax.ShapeDtypeStruct(table.shape, table.dtype),
            jax.ShapeDtypeStruct(state.shape, state.dtype),
        ),
        in_specs=[pl.BlockSpec(memory_space=pltpu.SMEM), vmem, vmem, vmem],
        out_specs=(pl.BlockSpec(memory_space=pl.ANY), vmem),
        scratch_shapes=[pltpu.SemaphoreType.DMA],
        name="write_table",
    )(touched, new_rows, state, table)


def per_device(
    lookup_block, lookup_offset, interaction_grad, table, adagrad_state, touched_blocks, dither
):
    micro_count, sample_count, feature_count, bag_count = lookup_block.shape
    n = lax.axis_size("mp")
    row_count, emb_width = table.shape
    touch_count = touched_blocks.shape[1]
    split = (micro_count, 2, feature_count // 2, bag_count, sample_count)
    blocks = lookup_block.transpose(0, 2, 3, 1).reshape(split)
    offsets = lookup_offset.transpose(0, 2, 3, 1).reshape(split)
    cot = interaction_grad.transpose(0, 2, 3, 1)
    table_blocks = table.reshape(row_count // BLOCK, BLOCK, emb_width)
    state = adagrad_state.reshape(row_count // (2 * BLOCK), 2 * BLOCK)
    new_rows, new_state = fused_step(
        n, blocks, offsets, cot, touched_blocks, state, table_blocks, dither[0]
    )
    new_rows = new_rows.reshape(touch_count, BLOCK, emb_width)
    new_table, new_state = write_table(touched_blocks, new_rows, new_state, table_blocks)
    return (new_table.reshape(row_count, emb_width), new_state.reshape(row_count))


def solution(mesh):
    return jax.shard_map(
        per_device,
        mesh=mesh,
        in_specs=(
            P(None, ("rep", "mp"), None, None),
            P(None, ("rep", "mp"), None, None),
            P(None, ("rep", "mp"), None, None),
            P("mp", None),
            P("mp"),
            P("mp", None),
            P("mp", None, None),
        ),
        out_specs=(P("mp", None), P("mp")),
        check_vma=False,
    )
```

```python
import functools
import math

import jax
import jax.numpy as jnp
from jax import lax
from jax.experimental import pallas as pl
from jax.experimental.pallas import tpu as pltpu
from jax.sharding import PartitionSpec as P

BLOCK = 64
LEARN_RATE = 0.1
POOL_DECAY = 0.5
DITHER_UNIT = 2.0 ** (-15)
SMALLEST = 2.0 ** (-14)
KEEP_BYTES = 8 << 20
MESH = pl.DeviceIdType.MESH


def dither_round(weights, dither_bits):
    magnitude = jnp.maximum(jnp.abs(weights), SMALLEST)
    spacing = jnp.exp2(jnp.floor(jnp.log2(magnitude)) - 7.0)
    grid_level = jnp.floor(weights / spacing + dither_bits.astype(jnp.float32) * DITHER_UNIT)
    return (grid_level * spacing).astype(jnp.bfloat16)


def step_kernel(
    n,
    block_hbm,
    offset_hbm,
    cot_ref,
    touched_ref,
    state_hbm,
    table_ref,
    dither_ref,
    out_ref,
    state_out_ref,
    block_ref,
    offset_ref,
    state_ref,
    rows_ref,
    cot_in,
    near,
    far,
    w_ref,
    w_other,
    table_in,
    dither_in,
    slab,
    slab_t,
    pooled_out,
    pooled_in,
    grad_out,
    grad_in,
    kept,
    total,
    squares,
    rows_new,
    small_sem,
    rows_send,
    near_recv,
    far_recv,
    pooled_send,
    pooled_recv,
    grad_send,
    grad_recv,
):
    me = lax.axis_index("mp")
    rep = lax.axis_index("rep")
    m = n // 2
    group = me // m
    local = lax.rem(me, m)
    mirror = lax.rem(me + m, n)
    samples = w_ref.shape[1]
    bags = rows_ref.shape[3]
    slab_size, width = slab.shape
    touch_count = slab_size // BLOCK
    keeps = kept.shape[2] == m
    columns = pl.ds(pl.multiple_of(rep * width, width), width)

    def at(peer):
        return {"device_id": (rep, peer), "device_id_type": MESH}

    partner = {"device_id": (1 - rep, me), "device_id_type": MESH}

    def each(first, body):
        def run(step, carry):
            body(lax.rem(local + step, m))
            return carry

        lax.fori_loop(first, m, run, 0)

    def near_at(j):
        return group * m + j

    def far_at(j):
        return (1 - group) * m + j

    barrier = pltpu.get_barrier_semaphore()
    each(1, lambda j: pl.semaphore_signal(barrier, inc=1, **at(near_at(j))))
    each(0, lambda j: pl.semaphore_signal(barrier, inc=1, **at(far_at(j))))
    pl.semaphore_signal(barrier, inc=1, **partner)
    block_copy = pltpu.make_async_copy(block_hbm, block_ref, small_sem.at[17])
    block_copy.start()
    offset_copy = pltpu.make_async_copy(offset_hbm, offset_ref, small_sem.at[18])
    offset_copy.start()
    state_copy = pltpu.make_async_copy(state_hbm, state_ref, small_sem.at[19])
    state_copy.start()
    table_copy = pltpu.make_async_copy(table_ref.at[:, :, columns], table_in, small_sem.at[13])
    table_copy.start()
    dither_copy = pltpu.make_async_copy(dither_ref.at[:, columns], dither_in, small_sem.at[14])
    dither_copy.start()
    block_copy.wait()
    offset_copy.wait()
    rows_ref[...] = block_ref[...] * BLOCK + offset_ref[...]
    near[rep, local] = rows_ref[:, :, local]
    total[...] = jnp.zeros_like(total)
    table_copy.wait()
    for block in range(touch_count):
        slab[block * BLOCK : (block + 1) * BLOCK, :] = table_in[touched_ref[0, block]]
    slab_t[0] = slab[...].astype(jnp.float32).T.astype(jnp.bfloat16)
    pl.semaphore_wait(barrier, n)

    def near_copy(j, slot):
        return pltpu.make_async_remote_copy(
            rows_ref.at[:, :, j],
            near.at[rep, slot],
            rows_send.at[0, j],
            near_recv.at[slot],
            **at(near_at(j)),
        )

    def far_copy(j, slot):
        return pltpu.make_async_remote_copy(
            rows_ref.at[:, 1 - group, j],
            far.at[rep, slot],
            rows_send.at[1, j],
            far_recv.at[slot],
            **at(far_at(j)),
        )

    each(1, lambda j: near_copy(j, local).start())
    slab_copy = pltpu.make_async_remote_copy(
        slab_t.at[0], slab_t.at[1], small_sem.at[9], small_sem.at[10], **at(mirror)
    )
    slab_copy.start()
    each(0, lambda j: far_copy(j, local).start())
    cot_size = cot_in.shape[1]

    def spread(chunk, carry):
        cot_copy = pltpu.make_async_copy(
            cot_ref.at[:, pl.ds(chunk * cot_size, cot_size)], cot_in, small_sem.at[0]
        )
        cot_copy.start()
        cot_copy.wait()
        for i in range(cot_size):
            pieces = [cot_in[micro, i].astype(jnp.float32) for micro in range(cot_in.shape[0])]
            at_row = pl.multiple_of((chunk * cot_size + i) * n, n)
            w_ref[pl.ds(at_row, n), :] = jnp.concatenate(pieces, axis=-1)
        return carry

    lax.fori_loop(0, n // cot_size, spread, 0)
    w_copy = pltpu.make_async_remote_copy(
        w_ref, w_other, small_sem.at[1], small_sem.at[2], **partner
    )
    w_copy.start()
    each(1, lambda j: near_copy(j, j).wait_recv())
    swap_near = pltpu.make_async_remote_copy(
        near.at[rep], near.at[rep], small_sem.at[3], small_sem.at[4], **partner
    )
    swap_near.start()

    offset_in_block = lax.broadcasted_iota(jnp.int32, (BLOCK, samples), 0)
    offset_in_block = offset_in_block.astype(jnp.float32).astype(jnp.bfloat16)
    one = jnp.ones((BLOCK, samples), jnp.bfloat16)

    def hits(micros):
        rows = jnp.concatenate([micros[i] for i in range(micros.shape[0])], axis=-1)
        blocks = []
        block_of, offset_of = rows // BLOCK, lax.rem(rows, BLOCK)
        for block in range(slab_size // BLOCK):
            wanted = jnp.where(block_of == block, offset_of, -1).astype(jnp.float32)
            counted = jnp.zeros((BLOCK, samples), jnp.bfloat16)
            for lookup in range(bags):
                row = jnp.broadcast_to(wanted[lookup : lookup + 1, :], (BLOCK, samples))
                same = row.astype(jnp.bfloat16) == offset_in_block
                counted = counted + jnp.where(same, one, jnp.zeros_like(one))
            blocks.append(counted)
        return jnp.concatenate(blocks, axis=0)

    def pooled_copy(part, which, j, slot):
        return pltpu.make_async_remote_copy(
            pooled_out.at[part, which, j],
            pooled_in.at[part, slot],
            pooled_send.at[part, which, j],
            pooled_recv.at[part, slot],
            **at(near_at(j)),
        )

    def grad_copy(part, peer, slot):
        return pltpu.make_async_remote_copy(
            grad_out.at[part, peer],
            grad_in.at[part, slot],
            grad_send.at[part, peer],
            grad_recv.at[part, slot],
            **at(peer),
        )

    def pool(part, replica, which):
        table = group if which == 0 else 1 - group
        feature = me if which == 0 else mirror

        def pooled(j):
            if which == 1 and keeps:
                counted = kept[1, part, j]
            else:
                counted = hits(near[replica, j, :, table])
                if keeps:
                    kept[0, part, j] = counted
            return jnp.dot(slab_t[which], counted, preferred_element_type=jnp.float32).astype(
                jnp.bfloat16
            )

        def send(j):
            pooled_out[part, which, j] = pooled(j)
            pooled_copy(part, which, j, feature).start()

        each(1, send)
        pooled_in[part, feature] = pooled(local)

    def interact(part, weights):
        def arrive(j):
            pooled_copy(part, 0, j, near_at(j)).wait_recv()
            pooled_copy(part, 1, j, far_at(j)).wait_recv()

        each(1, arrive)

        def mixed(feature):
            def add(other, carry):
                weight = (
                    weights[pl.ds(feature * n + other, 1), :]
                    + weights[pl.ds(other * n + feature, 1), :]
                )
                return carry + weight * pooled_in[part, other].astype(jnp.float32)

            start = POOL_DECAY * pooled_in[part, feature].astype(jnp.float32)
            return lax.fori_loop(0, n, add, start, unroll=4).astype(jnp.bfloat16)

        def send(peer):
            grad_out[part, peer] = mixed(peer)
            grad_copy(part, peer, me).start()

        each(0, lambda j: send(far_at(j)))
        each(1, lambda j: send(near_at(j)))
        grad_in[part, me] = mixed(me)

    def collect(part, replica):
        def add(peer, counted):
            total[...] += lax.dot_general(
                counted,
                grad_in[part, peer],
                (((1,), (1,)), ((), ())),
                preferred_element_type=jnp.float32,
            )

        def near_hits(j):
            return kept[0, part, j] if keeps else hits(near[replica, j, :, group])

        def take_near(j):
            grad_copy(part, near_at(j), near_at(j)).wait_recv()
            add(near_at(j), near_hits(j))

        def take_far(j):
            counted = hits(far[replica, j])
            grad_copy(part, far_at(j), far_at(j)).wait_recv()
            add(far_at(j), counted)

        add(me, near_hits(local))
        each(1, take_near)
        each(0, take_far)

    pool(0, rep, 0)
    swap_near.wait_recv()
    pool(1, 1 - rep, 0)
    each(0, lambda j: far_copy(j, j).wait_recv())
    swap_far = pltpu.make_async_remote_copy(
        far.at[rep], far.at[rep], small_sem.at[11], small_sem.at[12], **partner
    )
    swap_far.start()

    def keep_mirror(part, replica):
        def keep_one(j):
            kept[1, part, j] = hits(near[replica, j, :, 1 - group])

        each(0, keep_one)

    if keeps:
        keep_mirror(0, rep)
        keep_mirror(1, 1 - rep)
    slab_copy.wait_recv()
    pool(0, rep, 1)
    pool(1, 1 - rep, 1)
    interact(0, w_ref)
    w_copy.wait_recv()
    interact(1, w_other)
    collect(0, rep)
    swap_far.wait_recv()
    collect(1, 1 - rep)

    state_copy.wait()
    pieces = []
    for block in range(touch_count):
        at_block = touched_ref[0, block]
        pair = state_ref[pl.ds(at_block // 2, 1), :]
        pieces.append(jnp.where(lax.rem(at_block, 2) == 0, pair[:, :BLOCK], pair[:, BLOCK:]))
    state_row = jnp.concatenate(pieces, axis=1)
    grad = total[...]
    squares[0] = jnp.sum((grad * grad).T, axis=0, keepdims=True)
    square_copy = pltpu.make_async_remote_copy(
        squares.at[0], squares.at[1], small_sem.at[5], small_sem.at[6], **partner
    )
    square_copy.start()
    square_copy.wait_recv()
    first = jnp.where(rep == 0, squares[0], squares[1])
    second = jnp.where(rep == 0, squares[1], squares[0])
    state_next = state_row + (first + second) / (2.0 * width)
    divisor = jnp.broadcast_to(jnp.sqrt(state_next) + 1e-08, (width, slab_size)).T
    dither_copy.wait()
    size = slab_size // 2
    new_copies = []
    for piece in range(2):
        part = pl.ds(piece * size, size)
        span = slice(piece * size, (piece + 1) * size)
        moved = slab[span, :].astype(jnp.float32) - LEARN_RATE * total[span, :] / divisor[span]
        rows_new[0, span] = dither_round(moved, dither_in[span, :])
        new_copy = pltpu.make_async_remote_copy(
            rows_new.at[0, part],
            rows_new.at[1, part],
            small_sem.at[7 + 8 * piece],
            small_sem.at[8 + 8 * piece],
            **partner,
        )
        new_copy.start()
        new_copies.append(new_copy)
    out_ref[:, columns] = rows_new[0]
    state_all = state_ref[...]
    block_at = 2 * lax.broadcasted_iota(jnp.int32, state_all.shape, 0)
    block_at = block_at + lax.broadcasted_iota(jnp.int32, state_all.shape, 1) // BLOCK
    for block in range(touch_count):
        piece = state_next[:, block * BLOCK : (block + 1) * BLOCK]
        piece = jnp.broadcast_to(jnp.concatenate([piece, piece], axis=1), state_all.shape)
        state_all = jnp.where(block_at == touched_ref[0, block], piece, state_all)
    state_out_ref[...] = state_all

    each(1, lambda j: near_copy(j, j).wait_send())
    each(0, lambda j: far_copy(j, j).wait_send())
    for part in range(2):
        for which in range(2):
            each(1, lambda j: pooled_copy(part, which, j, j).wait_send())
        each(1, lambda j: grad_copy(part, near_at(j), me).wait_send())
        each(0, lambda j: grad_copy(part, far_at(j), me).wait_send())
    slab_copy.wait_send()
    w_copy.wait_send()
    swap_near.wait_send()
    swap_far.wait_send()
    square_copy.wait_send()
    for new_copy in new_copies:
        new_copy.wait()
    out_ref[:, pl.ds(pl.multiple_of((1 - rep) * width, width), width)] = rows_new[1]


def fused_step(n, blocks, offsets, cot, touched, state, table, dither):
    micros, sample_count = blocks.shape[0], blocks.shape[-1]
    samples = micros * sample_count
    cot_size = math.gcd(n, 16)
    slab_size, emb_width = dither.shape
    width = emb_width // 2
    m = n // 2
    keep = m if 8 * m * slab_size * samples <= KEEP_BYTES else 1
    dma = pltpu.SemaphoreType.DMA
    block = (2, n, width, samples)
    vmem = pl.BlockSpec(memory_space=pltpu.VMEM)
    smem = pl.BlockSpec(memory_space=pltpu.SMEM)
    hbm = pl.BlockSpec(memory_space=pltpu.HBM)
    return pl.pallas_call(
        functools.partial(step_kernel, n),
        out_shape=(
            jax.ShapeDtypeStruct((slab_size, emb_width), jnp.bfloat16),
            jax.ShapeDtypeStruct(state.shape, jnp.float32),
        ),
        in_specs=[hbm, hbm, hbm, smem, hbm, hbm, hbm],
        out_specs=(vmem, vmem),
        scratch_shapes=[
            pltpu.VMEM(blocks.shape, jnp.int32),
            pltpu.VMEM(blocks.shape, jnp.int32),
            pltpu.VMEM(state.shape, jnp.float32),
            pltpu.VMEM(blocks.shape, jnp.int32),
            pltpu.VMEM((micros, cot_size, n, sample_count), jnp.bfloat16),
            pltpu.VMEM((2, m, micros, 2) + blocks.shape[3:], jnp.int32),
            pltpu.VMEM((2, m, micros) + blocks.shape[3:], jnp.int32),
            pltpu.VMEM((n * n, samples), jnp.float32),
            pltpu.VMEM((n * n, samples), jnp.float32),
            pltpu.VMEM(table.shape[:2] + (width,), jnp.bfloat16),
            pltpu.VMEM((slab_size, width), jnp.int32),
            pltpu.VMEM((slab_size, width), jnp.bfloat16),
            pltpu.VMEM((2, width, slab_size), jnp.bfloat16),
            pltpu.VMEM((2, 2, m, width, samples), jnp.bfloat16),
            pltpu.VMEM(block, jnp.bfloat16),
            pltpu.VMEM(block, jnp.bfloat16),
            pltpu.VMEM(block, jnp.bfloat16),
            pltpu.VMEM((2, 2, keep, slab_size, samples), jnp.bfloat16),
            pltpu.VMEM((slab_size, width), jnp.float32),
            pltpu.VMEM((2, 1, slab_size), jnp.float32),
            pltpu.VMEM((2, slab_size, width), jnp.bfloat16),
            dma((20,)),
            dma((2, m)),
            dma((m,)),
            dma((m,)),
            dma((2, 2, m)),
            dma((2, n)),
            dma((2, n)),
            dma((2, n)),
        ],
        compiler_params=pltpu.CompilerParams(collective_id=0, has_side_effects=True),
        name="fused_step",
    )(blocks, offsets, cot, touched, state, table, dither)


def write_kernel(
    chunks, touched_ref, new_ref, state_ref, table_ref, out_ref, state_out_ref, held, read, write
):
    size = table_ref.shape[0] // chunks
    parts = [pl.ds(chunk * size, size) for chunk in range(chunks)]
    reads = [
        pltpu.make_async_copy(table_ref.at[part], held.at[part], read.at[chunk])
        for chunk, part in enumerate(parts)
    ]
    writes = [
        pltpu.make_async_copy(held.at[part], out_ref.at[part], write.at[chunk])
        for chunk, part in enumerate(parts)
    ]
    for copy in reads:
        copy.start()
    state_out_ref[...] = state_ref[...]
    for copy in reads:
        copy.wait()
    for block in range(touched_ref.shape[1]):
        held[touched_ref[0, block]] = new_ref[block]
    for copy in writes:
        copy.start()
    for copy in writes:
        copy.wait()


def write_table(touched, new_rows, state, table):
    chunks = math.gcd(table.shape[0], 4)
    hbm = pl.BlockSpec(memory_space=pl.ANY)
    vmem = pl.BlockSpec(memory_space=pltpu.VMEM)
    return pl.pallas_call(
        functools.partial(write_kernel, chunks),
        out_shape=(
            jax.ShapeDtypeStruct(table.shape, table.dtype),
            jax.ShapeDtypeStruct(state.shape, state.dtype),
        ),
        in_specs=[pl.BlockSpec(memory_space=pltpu.SMEM), vmem, vmem, hbm],
        out_specs=(hbm, vmem),
        scratch_shapes=[
            pltpu.VMEM(table.shape, table.dtype),
            pltpu.SemaphoreType.DMA((chunks,)),
            pltpu.SemaphoreType.DMA((chunks,)),
        ],
        name="write_table",
    )(touched, new_rows, state, table)


def per_device(
    lookup_block, lookup_offset, interaction_grad, table, adagrad_state, touched_blocks, dither
):
    micro_count, sample_count, feature_count, bag_count = lookup_block.shape
    n = lax.axis_size("mp")
    row_count, emb_width = table.shape
    touch_count = touched_blocks.shape[1]
    split = (micro_count, 2, feature_count // 2, bag_count, sample_count)
    blocks = lookup_block.transpose(0, 2, 3, 1).reshape(split)
    offsets = lookup_offset.transpose(0, 2, 3, 1).reshape(split)
    cot = interaction_grad.transpose(0, 2, 3, 1)
    table_blocks = table.reshape(row_count // BLOCK, BLOCK, emb_width)
    state = adagrad_state.reshape(row_count // (2 * BLOCK), 2 * BLOCK)
    new_rows, new_state = fused_step(
        n, blocks, offsets, cot, touched_blocks, state, table_blocks, dither[0]
    )
    new_rows = new_rows.reshape(touch_count, BLOCK, emb_width)
    new_table, new_state = write_table(touched_blocks, new_rows, new_state, table_blocks)
    return (new_table.reshape(row_count, emb_width), new_state.reshape(row_count))


def solution(mesh):
    return jax.shard_map(
        per_device,
        mesh=mesh,
        in_specs=(
            P(None, ("rep", "mp"), None, None),
            P(None, ("rep", "mp"), None, None),
            P(None, ("rep", "mp"), None, None),
            P("mp", None),
            P("mp"),
            P("mp", None),
            P("mp", None, None),
        ),
        out_specs=(P("mp", None), P("mp")),
        check_vma=False,
    )
```

```python
import functools
import math

import jax
import jax.numpy as jnp
from jax import lax
from jax.experimental import pallas as pl
from jax.experimental.pallas import tpu as pltpu
from jax.sharding import PartitionSpec as P

BLOCK = 64
LEARN_RATE = 0.1
POOL_DECAY = 0.5
DITHER_UNIT = 2.0 ** (-15)
SMALLEST = 2.0 ** (-14)
KEEP_BYTES = 8 << 20
MESH = pl.DeviceIdType.MESH


def dither_round(weights, dither_bits):
    magnitude = jnp.maximum(jnp.abs(weights), SMALLEST)
    spacing = jnp.exp2(jnp.floor(jnp.log2(magnitude)) - 7.0)
    grid_level = jnp.floor(weights / spacing + dither_bits.astype(jnp.float32) * DITHER_UNIT)
    return (grid_level * spacing).astype(jnp.bfloat16)


def step_kernel(
    n,
    block_hbm,
    offset_hbm,
    cot_ref,
    touched_ref,
    state_hbm,
    table_ref,
    dither_ref,
    out_ref,
    state_out_ref,
    block_ref,
    offset_ref,
    state_ref,
    rows_ref,
    cot_in,
    near,
    far,
    w_ref,
    w_other,
    table_in,
    dither_in,
    slab,
    slab_t,
    pooled_out,
    pooled_in,
    grad_out,
    grad_in,
    kept,
    total,
    squares,
    rows_new,
    small_sem,
    rows_send,
    near_recv,
    far_recv,
    pooled_send,
    pooled_recv,
    grad_send,
    grad_recv,
):
    me = lax.axis_index("mp")
    rep = lax.axis_index("rep")
    m = n // 2
    group = me // m
    local = lax.rem(me, m)
    mirror = lax.rem(me + m, n)
    samples = w_ref.shape[1]
    bags = rows_ref.shape[3]
    slab_size, width = slab.shape
    touch_count = slab_size // BLOCK
    keeps = kept.shape[1] == m
    columns = pl.ds(pl.multiple_of(rep * width, width), width)

    def at(peer):
        return {"device_id": (rep, peer), "device_id_type": MESH}

    partner = {"device_id": (1 - rep, me), "device_id_type": MESH}

    def each(first, body):
        def run(step, carry):
            body(lax.rem(local + step, m))
            return carry

        lax.fori_loop(first, m, run, 0)

    def near_at(j):
        return group * m + j

    def far_at(j):
        return (1 - group) * m + j

    barrier = pltpu.get_barrier_semaphore()
    each(1, lambda j: pl.semaphore_signal(barrier, inc=1, **at(near_at(j))))
    each(0, lambda j: pl.semaphore_signal(barrier, inc=1, **at(far_at(j))))
    pl.semaphore_signal(barrier, inc=1, **partner)
    block_copy = pltpu.make_async_copy(block_hbm, block_ref, small_sem.at[17])
    block_copy.start()
    offset_copy = pltpu.make_async_copy(offset_hbm, offset_ref, small_sem.at[18])
    offset_copy.start()
    state_copy = pltpu.make_async_copy(state_hbm, state_ref, small_sem.at[19])
    state_copy.start()
    table_copy = pltpu.make_async_copy(table_ref.at[:, :, columns], table_in, small_sem.at[13])
    table_copy.start()
    dither_copy = pltpu.make_async_copy(dither_ref.at[:, columns], dither_in, small_sem.at[14])
    dither_copy.start()
    block_copy.wait()
    offset_copy.wait()
    rows_ref[...] = block_ref[...] * BLOCK + offset_ref[...]
    near[rep, local] = rows_ref[:, :, local]
    total[...] = jnp.zeros_like(total)
    table_copy.wait()
    for block in range(touch_count):
        slab[block * BLOCK : (block + 1) * BLOCK, :] = table_in[touched_ref[0, block]]
    slab_t[0] = slab[...].astype(jnp.float32).T.astype(jnp.bfloat16)
    pl.semaphore_wait(barrier, n)

    def near_copy(j, slot):
        return pltpu.make_async_remote_copy(
            rows_ref.at[:, :, j],
            near.at[rep, slot],
            rows_send.at[0, j],
            near_recv.at[slot],
            **at(near_at(j)),
        )

    def far_copy(j, slot):
        return pltpu.make_async_remote_copy(
            rows_ref.at[:, 1 - group, j],
            far.at[rep, slot],
            rows_send.at[1, j],
            far_recv.at[slot],
            **at(far_at(j)),
        )

    each(1, lambda j: near_copy(j, local).start())
    slab_copy = pltpu.make_async_remote_copy(
        slab_t.at[0], slab_t.at[1], small_sem.at[9], small_sem.at[10], **at(mirror)
    )
    slab_copy.start()
    each(0, lambda j: far_copy(j, local).start())
    cot_size = cot_in.shape[1]

    def spread(chunk, carry):
        cot_copy = pltpu.make_async_copy(
            cot_ref.at[:, pl.ds(chunk * cot_size, cot_size)], cot_in, small_sem.at[0]
        )
        cot_copy.start()
        cot_copy.wait()
        for i in range(cot_size):
            pieces = [cot_in[micro, i].astype(jnp.float32) for micro in range(cot_in.shape[0])]
            at_row = pl.multiple_of((chunk * cot_size + i) * n, n)
            w_ref[pl.ds(at_row, n), :] = jnp.concatenate(pieces, axis=-1)
        return carry

    lax.fori_loop(0, n // cot_size, spread, 0)
    w_copy = pltpu.make_async_remote_copy(
        w_ref, w_other, small_sem.at[1], small_sem.at[2], **partner
    )
    w_copy.start()
    each(1, lambda j: near_copy(j, j).wait_recv())
    swap_near = pltpu.make_async_remote_copy(
        near.at[rep], near.at[rep], small_sem.at[3], small_sem.at[4], **partner
    )
    swap_near.start()

    offset_in_block = lax.broadcasted_iota(jnp.int32, (BLOCK, samples), 0)
    offset_in_block = offset_in_block.astype(jnp.float32).astype(jnp.bfloat16)
    one = jnp.ones((BLOCK, samples), jnp.bfloat16)

    def hits(micros):
        rows = jnp.concatenate([micros[i] for i in range(micros.shape[0])], axis=-1)
        blocks = []
        block_of, offset_of = rows // BLOCK, lax.rem(rows, BLOCK)
        for block in range(slab_size // BLOCK):
            wanted = jnp.where(block_of == block, offset_of, -1).astype(jnp.float32)
            counted = jnp.zeros((BLOCK, samples), jnp.bfloat16)
            for lookup in range(bags):
                row = jnp.broadcast_to(wanted[lookup : lookup + 1, :], (BLOCK, samples))
                same = row.astype(jnp.bfloat16) == offset_in_block
                counted = counted + jnp.where(same, one, jnp.zeros_like(one))
            blocks.append(counted)
        return jnp.concatenate(blocks, axis=0)

    def pooled_copy(part, which, j, slot):
        return pltpu.make_async_remote_copy(
            pooled_out.at[part, which, j],
            pooled_in.at[part, slot],
            pooled_send.at[part, which, j],
            pooled_recv.at[part, slot],
            **at(near_at(j)),
        )

    def grad_copy(part, peer, slot):
        return pltpu.make_async_remote_copy(
            grad_out.at[part, peer],
            grad_in.at[part, slot],
            grad_send.at[part, peer],
            grad_recv.at[part, slot],
            **at(peer),
        )

    def pool(part, replica, which):
        table = group if which == 0 else 1 - group
        feature = me if which == 0 else mirror

        def pooled(j):
            counted = hits(near[replica, j, :, table])
            if which == 0 and keeps:
                kept[part, j] = counted
            return jnp.dot(slab_t[which], counted, preferred_element_type=jnp.float32).astype(
                jnp.bfloat16
            )

        def send(j):
            pooled_out[part, which, j] = pooled(j)
            pooled_copy(part, which, j, feature).start()

        each(1, send)
        pooled_in[part, feature] = pooled(local)

    def interact(part, weights):
        def arrive(j):
            pooled_copy(part, 0, j, near_at(j)).wait_recv()
            pooled_copy(part, 1, j, far_at(j)).wait_recv()

        each(1, arrive)

        def mixed(feature):
            def add(other, carry):
                weight = (
                    weights[pl.ds(feature * n + other, 1), :]
                    + weights[pl.ds(other * n + feature, 1), :]
                )
                return carry + weight * pooled_in[part, other].astype(jnp.float32)

            start = POOL_DECAY * pooled_in[part, feature].astype(jnp.float32)
            return lax.fori_loop(0, n, add, start, unroll=4).astype(jnp.bfloat16)

        def send(peer):
            grad_out[part, peer] = mixed(peer)
            grad_copy(part, peer, me).start()

        each(0, lambda j: send(far_at(j)))
        each(1, lambda j: send(near_at(j)))
        grad_in[part, me] = mixed(me)

    def collect(part, replica):
        def add(peer, counted):
            total[...] += lax.dot_general(
                counted,
                grad_in[part, peer],
                (((1,), (1,)), ((), ())),
                preferred_element_type=jnp.float32,
            )

        def near_hits(j):
            return kept[part, j] if keeps else hits(near[replica, j, :, group])

        def take_near(j):
            grad_copy(part, near_at(j), near_at(j)).wait_recv()
            add(near_at(j), near_hits(j))

        def take_far(j):
            counted = hits(far[replica, j])
            grad_copy(part, far_at(j), far_at(j)).wait_recv()
            add(far_at(j), counted)

        add(me, near_hits(local))
        each(1, take_near)
        each(0, take_far)

    pool(0, rep, 0)
    slab_copy.wait_recv()
    pool(0, rep, 1)
    swap_near.wait_recv()
    pool(1, 1 - rep, 0)
    interact(0, w_ref)
    pool(1, 1 - rep, 1)
    each(0, lambda j: far_copy(j, j).wait_recv())
    swap_far = pltpu.make_async_remote_copy(
        far.at[rep], far.at[rep], small_sem.at[11], small_sem.at[12], **partner
    )
    swap_far.start()
    w_copy.wait_recv()
    interact(1, w_other)
    collect(0, rep)
    swap_far.wait_recv()
    collect(1, 1 - rep)

    state_copy.wait()
    pieces = []
    for block in range(touch_count):
        at_block = touched_ref[0, block]
        pair = state_ref[pl.ds(at_block // 2, 1), :]
        pieces.append(jnp.where(lax.rem(at_block, 2) == 0, pair[:, :BLOCK], pair[:, BLOCK:]))
    state_row = jnp.concatenate(pieces, axis=1)
    grad = total[...]
    squares[0] = jnp.sum((grad * grad).T, axis=0, keepdims=True)
    square_copy = pltpu.make_async_remote_copy(
        squares.at[0], squares.at[1], small_sem.at[5], small_sem.at[6], **partner
    )
    square_copy.start()
    square_copy.wait_recv()
    first = jnp.where(rep == 0, squares[0], squares[1])
    second = jnp.where(rep == 0, squares[1], squares[0])
    state_next = state_row + (first + second) / (2.0 * width)
    divisor = jnp.broadcast_to(jnp.sqrt(state_next) + 1e-08, (width, slab_size)).T
    dither_copy.wait()
    size = slab_size // 2
    new_copies = []
    for piece in range(2):
        part = pl.ds(piece * size, size)
        span = slice(piece * size, (piece + 1) * size)
        moved = slab[span, :].astype(jnp.float32) - LEARN_RATE * total[span, :] / divisor[span]
        rows_new[0, span] = dither_round(moved, dither_in[span, :])
        new_copy = pltpu.make_async_remote_copy(
            rows_new.at[0, part],
            rows_new.at[1, part],
            small_sem.at[7 + 8 * piece],
            small_sem.at[8 + 8 * piece],
            **partner,
        )
        new_copy.start()
        new_copies.append(new_copy)
    out_ref[:, columns] = rows_new[0]
    state_all = state_ref[...]
    block_at = 2 * lax.broadcasted_iota(jnp.int32, state_all.shape, 0)
    block_at = block_at + lax.broadcasted_iota(jnp.int32, state_all.shape, 1) // BLOCK
    for block in range(touch_count):
        piece = state_next[:, block * BLOCK : (block + 1) * BLOCK]
        piece = jnp.broadcast_to(jnp.concatenate([piece, piece], axis=1), state_all.shape)
        state_all = jnp.where(block_at == touched_ref[0, block], piece, state_all)
    state_out_ref[...] = state_all

    each(1, lambda j: near_copy(j, j).wait_send())
    each(0, lambda j: far_copy(j, j).wait_send())
    for part in range(2):
        for which in range(2):
            each(1, lambda j: pooled_copy(part, which, j, j).wait_send())
        each(1, lambda j: grad_copy(part, near_at(j), me).wait_send())
        each(0, lambda j: grad_copy(part, far_at(j), me).wait_send())
    slab_copy.wait_send()
    w_copy.wait_send()
    swap_near.wait_send()
    swap_far.wait_send()
    square_copy.wait_send()
    for new_copy in new_copies:
        new_copy.wait()
    out_ref[:, pl.ds(pl.multiple_of((1 - rep) * width, width), width)] = rows_new[1]


def fused_step(n, blocks, offsets, cot, touched, state, table, dither):
    micros, sample_count = blocks.shape[0], blocks.shape[-1]
    samples = micros * sample_count
    cot_size = math.gcd(n, 16)
    slab_size, emb_width = dither.shape
    width = emb_width // 2
    m = n // 2
    keep = m if 4 * m * slab_size * samples <= KEEP_BYTES else 1
    dma = pltpu.SemaphoreType.DMA
    block = (2, n, width, samples)
    vmem = pl.BlockSpec(memory_space=pltpu.VMEM)
    smem = pl.BlockSpec(memory_space=pltpu.SMEM)
    hbm = pl.BlockSpec(memory_space=pltpu.HBM)
    return pl.pallas_call(
        functools.partial(step_kernel, n),
        out_shape=(
            jax.ShapeDtypeStruct((slab_size, emb_width), jnp.bfloat16),
            jax.ShapeDtypeStruct(state.shape, jnp.float32),
        ),
        in_specs=[hbm, hbm, hbm, smem, hbm, hbm, hbm],
        out_specs=(vmem, vmem),
        scratch_shapes=[
            pltpu.VMEM(blocks.shape, jnp.int32),
            pltpu.VMEM(blocks.shape, jnp.int32),
            pltpu.VMEM(state.shape, jnp.float32),
            pltpu.VMEM(blocks.shape, jnp.int32),
            pltpu.VMEM((micros, cot_size, n, sample_count), jnp.bfloat16),
            pltpu.VMEM((2, m, micros, 2) + blocks.shape[3:], jnp.int32),
            pltpu.VMEM((2, m, micros) + blocks.shape[3:], jnp.int32),
            pltpu.VMEM((n * n, samples), jnp.float32),
            pltpu.VMEM((n * n, samples), jnp.float32),
            pltpu.VMEM(table.shape[:2] + (width,), jnp.bfloat16),
            pltpu.VMEM((slab_size, width), jnp.int32),
            pltpu.VMEM((slab_size, width), jnp.bfloat16),
            pltpu.VMEM((2, width, slab_size), jnp.bfloat16),
            pltpu.VMEM((2, 2, m, width, samples), jnp.bfloat16),
            pltpu.VMEM(block, jnp.bfloat16),
            pltpu.VMEM(block, jnp.bfloat16),
            pltpu.VMEM(block, jnp.bfloat16),
            pltpu.VMEM((2, keep, slab_size, samples), jnp.bfloat16),
            pltpu.VMEM((slab_size, width), jnp.float32),
            pltpu.VMEM((2, 1, slab_size), jnp.float32),
            pltpu.VMEM((2, slab_size, width), jnp.bfloat16),
            dma((20,)),
            dma((2, m)),
            dma((m,)),
            dma((m,)),
            dma((2, 2, m)),
            dma((2, n)),
            dma((2, n)),
            dma((2, n)),
        ],
        compiler_params=pltpu.CompilerParams(collective_id=0, has_side_effects=True),
        name="fused_step",
    )(blocks, offsets, cot, touched, state, table, dither)


def write_kernel(touched_ref, new_ref, state_ref, table_ref, out_ref, state_out_ref, sem):
    state_out_ref[...] = state_ref[...]

    def write(block, carry):
        new = -1
        for i in range(touched_ref.shape[1]):
            new = jnp.where(touched_ref[0, i] == block, i, new)

        @pl.when(new >= 0)
        def _():
            pltpu.make_async_copy(new_ref.at[new], out_ref.at[block], sem).start()

        @pl.when(new < 0)
        def _():
            pltpu.make_async_copy(table_ref.at[block], out_ref.at[block], sem).start()

        return carry

    lax.fori_loop(0, table_ref.shape[0], write, 0)
    pltpu.make_async_copy(table_ref, out_ref, sem).wait()


def write_table(touched, new_rows, state, table):
    vmem = pl.BlockSpec(memory_space=pltpu.VMEM)
    return pl.pallas_call(
        write_kernel,
        out_shape=(
            jax.ShapeDtypeStruct(table.shape, table.dtype),
            jax.ShapeDtypeStruct(state.shape, state.dtype),
        ),
        in_specs=[pl.BlockSpec(memory_space=pltpu.SMEM), vmem, vmem, vmem],
        out_specs=(pl.BlockSpec(memory_space=pl.ANY), vmem),
        scratch_shapes=[pltpu.SemaphoreType.DMA],
        name="write_table",
    )(touched, new_rows, state, table)


def per_device(
    lookup_block, lookup_offset, interaction_grad, table, adagrad_state, touched_blocks, dither
):
    micro_count, sample_count, feature_count, bag_count = lookup_block.shape
    n = lax.axis_size("mp")
    row_count, emb_width = table.shape
    touch_count = touched_blocks.shape[1]
    split = (micro_count, 2, feature_count // 2, bag_count, sample_count)
    blocks = lookup_block.transpose(0, 2, 3, 1).reshape(split)
    offsets = lookup_offset.transpose(0, 2, 3, 1).reshape(split)
    cot = interaction_grad.transpose(0, 2, 3, 1)
    table_blocks = table.reshape(row_count // BLOCK, BLOCK, emb_width)
    state = adagrad_state.reshape(row_count // (2 * BLOCK), 2 * BLOCK)
    new_rows, new_state = fused_step(
        n, blocks, offsets, cot, touched_blocks, state, table_blocks, dither[0]
    )
    new_rows = new_rows.reshape(touch_count, BLOCK, emb_width)
    new_table, new_state = write_table(touched_blocks, new_rows, new_state, table_blocks)
    return (new_table.reshape(row_count, emb_width), new_state.reshape(row_count))


def solution(mesh):
    return jax.shard_map(
        per_device,
        mesh=mesh,
        in_specs=(
            P(None, ("rep", "mp"), None, None),
            P(None, ("rep", "mp"), None, None),
            P(None, ("rep", "mp"), None, None),
            P("mp", None),
            P("mp"),
            P("mp", None),
            P("mp", None, None),
        ),
        out_specs=(P("mp", None), P("mp")),
        check_vma=False,
    )
```
